128 devices in a mesh: gx: 8 (over x, z_lo), gy: 16 (over z_hi, y, core).
Axes of the slice: x: 4, y: 4, z: 4 (z_hi: 2, z_lo: 2; z = z_hi * 2 + z_lo), core: 2. Of those that a mesh axis runs over, the one named last changes fastest.
Arguments:
- state: float32 [8, 8, 128, 2048], P(None, None, 'gx', 'gy'), may hold values from -3 to 3
- residual: float32 [128], replicated, may hold values from -2.5 to 2.5
- shift_rows: int32 [128], P('gx'), may hold values from 0 to 2047
- shear_offset: int32 [1], replicated, may hold values from 0 to 2047
Outputs:
- evolved: float32 [8, 8, 128, 2048], P(None, None, 'gx', 'gy')
The draws below stay inside these ranges and needn't reach their ends.
Inputs may be any that keep to these rules, and one draw needn't show every extreme that they name: `shift_rows`: each row's whole-cell displacement; it wraps around the 2048 azimuthal cells. `shear_offset`: whole-cell offset of the sheared radial boundary.
All inputs are finite; a program needn't handle non-finite values.
Results may differ from the reference program's by a relative error of at most 0.00002.
Values sent between devices are 32-bit elements; how exact they have to be, the bound alone decides.
No kernel may reach another device: no remote copies, remote signals or barrier semaphores. Data moves between devices by JAX's collectives and lax.ppermute only.
A program may use at most 128 MiB of HBM per device.

```python
import jax
import jax.numpy as jnp

NZ = 8
NX = 128
NY = 2048


def plant(result, own_key, least, high):
    spot = [jax.random.randint(jax.random.fold_in(own_key, axis), (), 0, length) for axis, length in enumerate(result.shape)]
    widest = result.shape.index(max(result.shape))
    neighbour = spot[:widest] + [(spot[widest] + 1) % result.shape[widest]] + spot[widest + 1:]
    return result.at[tuple(spot)].set(least).at[tuple(neighbour)].set(high)


def steps_of(key, extent, shards, low, high):
    level, own = 1.0, jax.random.fold_in(key, 6)
    for position, shards_of in shards:
        heights = jnp.exp(jax.random.uniform(jax.random.fold_in(own, position), (shards_of,), jnp.float32, low / len(shards), high / len(shards)))
        level = level * jnp.repeat(heights, extent[position] // shards_of).reshape([-1 if axis == position else 1 for axis in range(len(extent))])
    return level


def noise(rng, extent, spread, reach, cuts=(), held_as=jnp.bfloat16):
    result = spread * jax.random.normal(rng, extent, jnp.float32)
    if cuts:
        result = result * steps_of(rng, extent, cuts, -0.22, 0.18)
    return jnp.clip(result, -reach, reach).astype(held_as)


def setup_inputs(seed: int = 0) -> dict:
    key_of = jax.random.split(jax.random.key(seed), 5)
    return {
        "state": noise(key_of[0], (8, NZ, NX, NY), 0.5, 3.0, ((2, 8), (3, 16)), jnp.float32),
        "residual": jnp.clip(jax.random.uniform(key_of[1], (NX,), jnp.float32, -2.5, 2.5), -2.5, 2.5),
        "shift_rows": plant(jax.random.randint(key_of[2], (NX,), 0, NY), jax.random.fold_in(key_of[2], 1), 0, NY - 1).astype(jnp.int32),
        "shear_offset": jax.random.randint(key_of[3], (1,), 0, NY).astype(jnp.int32),
    }


time_step = 0.2
viscous = 0.1
resist = 0.1
sound_sq = 1.0
rotation = 0.5
shear_rate = 1.5


def ahead(field, dimension):
    return jnp.roll(field, -1, dimension)


def behind(field, dimension):
    return jnp.roll(field, 1, dimension)


def deriv(field, dimension):
    return 0.5 * (ahead(field, dimension) - behind(field, dimension))


def laplace(field):
    total = -6.0 * field
    for dimension in range(3):
        total = total + ahead(field, dimension) + behind(field, dimension)
    return total


def pair_mean(field, first_dim, second_dim):
    back_one = behind(field, first_dim)
    return 0.25 * (field + back_one + behind(field, second_dim) + behind(back_one, second_dim))


def rates(state, residual):
    log_rho, vel_x, vel_y, vel_z, entropy, mag_x, mag_y, mag_z = state
    drift = vel_y + residual[None, :, None]

    def advect(field):
        return vel_x * deriv(field, 1) + drift * deriv(field, 2) + vel_z * deriv(field, 0)

    cell_x = 0.5 * (mag_x + ahead(mag_x, 1))
    cell_y = 0.5 * (mag_y + ahead(mag_y, 2))
    cell_z = 0.5 * (mag_z + ahead(mag_z, 0))
    cur_x = deriv(cell_z, 2) - deriv(cell_y, 0)
    cur_y = deriv(cell_x, 0) - deriv(cell_z, 1)
    cur_z = deriv(cell_y, 1) - deriv(cell_x, 2)
    inverse = jnp.exp(-log_rho)
    force_x = inverse * (cur_y * cell_z - cur_z * cell_y)
    force_y = inverse * (cur_z * cell_x - cur_x * cell_z)
    force_z = inverse * (cur_x * cell_y - cur_y * cell_x)
    rate_rho = -advect(log_rho) - (deriv(vel_x, 1) + deriv(vel_y, 2) + deriv(vel_z, 0)) + viscous * laplace(log_rho)
    rate_vx = -advect(vel_x) - sound_sq * (deriv(log_rho, 1) + deriv(entropy, 1)) + force_x + viscous * laplace(vel_x) + 2.0 * rotation * vel_y
    rate_vy = -advect(vel_y) - sound_sq * (deriv(log_rho, 2) + deriv(entropy, 2)) + force_y + viscous * laplace(vel_y) - (2.0 - shear_rate) * rotation * vel_x
    rate_vz = -advect(vel_z) - sound_sq * (deriv(log_rho, 0) + deriv(entropy, 0)) + force_z + viscous * laplace(vel_z)
    rate_ent = -advect(entropy) + viscous * laplace(entropy) + resist * inverse * (cur_x * cur_x + cur_y * cur_y + cur_z * cur_z)
    emf_z = -(pair_mean(vel_x, 1, 2) * 0.5 * (mag_y + behind(mag_y, 1)) - pair_mean(drift, 1, 2) * 0.5 * (mag_x + behind(mag_x, 2))) + resist * ((mag_y - behind(mag_y, 1)) - (mag_x - behind(mag_x, 2)))
    emf_x = -(pair_mean(drift, 2, 0) * 0.5 * (mag_z + behind(mag_z, 2)) - pair_mean(vel_z, 2, 0) * 0.5 * (mag_y + behind(mag_y, 0))) + resist * ((mag_z - behind(mag_z, 2)) - (mag_y - behind(mag_y, 0)))
    emf_y = -(pair_mean(vel_z, 1, 0) * 0.5 * (mag_x + behind(mag_x, 0)) - pair_mean(vel_x, 1, 0) * 0.5 * (mag_z + behind(mag_z, 1))) + resist * ((mag_x - behind(mag_x, 0)) - (mag_z - behind(mag_z, 1)))
    back_y = behind(mag_x, 2)
    stretch = 0.25 * (mag_x + ahead(mag_x, 1) + back_y + ahead(back_y, 1))
    rate_bx = -(ahead(emf_z, 2) - emf_z) + (ahead(emf_y, 0) - emf_y)
    rate_by = -(ahead(emf_x, 0) - emf_x) + (ahead(emf_z, 1) - emf_z) - shear_rate * rotation * stretch
    rate_bz = -(ahead(emf_y, 1) - emf_y) + (ahead(emf_x, 2) - emf_x)
    return jnp.stack([rate_rho, rate_vx, rate_vy, rate_vz, rate_ent, rate_bx, rate_by, rate_bz])


def crop(field, depth):
    return field[..., depth:-depth, depth:-depth]


def reference(state, residual, shift_rows, shear_offset):
    cells_y = state.shape[3]
    columns = jnp.arange(cells_y, dtype=jnp.int32)
    source = (columns[None, :] - shift_rows[:, None]) % cells_y
    moved = jnp.take_along_axis(state, source[None, None], axis=3)
    offset = shear_offset[0]

    def extend(field):
        lower = jnp.roll(field[:, :, -2:, :], -offset, 3)
        upper = jnp.roll(field[:, :, :2, :], offset, 3)
        wide = jnp.concatenate([lower, field, upper], 2)
        return jnp.concatenate([wide[..., -2:], wide, wide[..., :2]], 3)

    drift_rows = jnp.concatenate([residual[-2:], residual, residual[:2]])
    first = moved + time_step * crop(rates(extend(moved), drift_rows), 2)
    second = first + time_step * crop(rates(extend(first), drift_rows), 2)
    return 0.5 * (moved + second)
```

```python
import jax
import jax.numpy as jnp
from jax import lax
from jax.experimental import pallas as pl
from jax.experimental.pallas import tpu as pltpu
from jax.sharding import PartitionSpec as P

time_step = 0.2
viscous = 0.1
resist = 0.1
sound_sq = 1.0
rotation = 0.5
shear_rate = 1.5

LANES = 128
DEPTH = 2
STRIP = 4 * DEPTH


def passed_along(value, axis, steps):
    count = lax.axis_size(axis)
    pairs = [(source, (source + steps) % count) for source in range(count)]
    return lax.ppermute(value, axis, pairs)


def turn_lines(groups, rows, planes):
    own = rows * planes
    ghost = DEPTH * planes
    total = own + 2 * ghost
    wide = rows + 2 * DEPTH
    pitch = wide + 2

    def kernel(shifts, mine, low, high, out, lines, sems):
        copies = []
        for part, (source, start, size) in enumerate(
            ((mine, 0, own), (low, own, ghost), (high, own + ghost, ghost))
        ):
            for turn, (first, count, target) in enumerate(
                ((0, groups, 1), (0, groups, groups + 1), (groups - 1, 1, 0))
            ):
                copies.append(
                    pltpu.make_async_copy(
                        source.at[pl.ds(first, count)],
                        lines.at[pl.ds(target, count), pl.ds(start, size)],
                        sems.at[part, turn],
                    )
                )
        for copy in copies:
            copy.start()
        for copy in copies:
            copy.wait()
        flat = lines.reshape((2 * groups + 1) * total, LANES)
        lane = lax.broadcasted_iota(jnp.int32, (groups, LANES), 1)
        strips = [[jnp.zeros((groups, LANES), jnp.float32) for _ in range(planes)] for _ in range(2)]
        for row in range(wide):
            amount = shifts[row]
            block = (groups - amount // LANES) % groups
            part = amount % LANES
            keep = lane < LANES - part
            edge = ((lane + part) & (LANES - 1)) < 2 * DEPTH
            place = row // 2
            strip_turn = (part + 2 * DEPTH + STRIP * place) % LANES
            in_place = (lane >= STRIP * place) & (lane < STRIP * (place + 1))
            for plane in range(planes):
                if row < DEPTH:
                    line = own + plane * DEPTH + row
                elif row < DEPTH + rows:
                    line = plane * rows + row - DEPTH
                else:
                    line = own + ghost + plane * DEPTH + row - DEPTH - rows
                before, here, after = (
                    flat[pl.ds((block + ahead_by) * total + line, groups, stride=total), :]
                    for ahead_by in range(3)
                )
                window = jnp.where(keep, here, before)
                out[pl.ds(plane * pitch + row, groups, stride=planes * pitch), :] = pltpu.roll(
                    window, part, 1
                )
                rim = jnp.where(edge, jnp.where(keep, after, here), window)
                strips[row % 2][plane] = jnp.where(
                    in_place, pltpu.roll(rim, strip_turn, 1), strips[row % 2][plane]
                )
        for parity in range(2):
            for plane in range(planes):
                out[pl.ds(plane * pitch + wide + parity, groups, stride=planes * pitch), :] = strips[
                    parity
                ][plane]

    return pl.pallas_call(
        kernel,
        in_specs=[pl.BlockSpec(memory_space=pltpu.SMEM)] + [pl.BlockSpec(memory_space=pl.ANY)] * 3,
        out_shape=jax.ShapeDtypeStruct((groups * planes * pitch, LANES), jnp.float32),
        out_specs=pl.BlockSpec(memory_space=pltpu.VMEM),
        scratch_shapes=[
            pltpu.VMEM((2 * groups + 1, total, LANES), jnp.float32),
            pltpu.SemaphoreType.DMA((3, 3)),
        ],
        compiler_params=pltpu.CompilerParams(vmem_limit_bytes=24 * 1024 * 1024),
        name="turn_lines",
    )


def y_up(tile):
    return pltpu.roll(tile, LANES - 1, 1)


def y_dn(tile):
    return pltpu.roll(tile, 1, 1)


def z_up(tile):
    return pltpu.roll(tile, tile.shape[0] - 1, 0)


def z_dn(tile):
    return pltpu.roll(tile, 1, 0)


def radial_edges(prev, here, drift_prev, drift):
    _, vel_x, _, vel_z, _, mag_x, mag_y, mag_z = here
    two_x = vel_x + prev[1]
    two_z = vel_z + prev[3]
    two_w = drift + drift_prev
    mag_x_y = y_dn(mag_x)
    mag_x_z = z_dn(mag_x)
    emf_z = 0.125 * (
        (two_w + y_dn(two_w)) * (mag_x + mag_x_y) - (two_x + y_dn(two_x)) * (mag_y + prev[6])
    ) + resist * ((mag_y - prev[6]) - (mag_x - mag_x_y))
    emf_y = 0.125 * (
        (two_x + z_dn(two_x)) * (mag_z + prev[7]) - (two_z + z_dn(two_z)) * (mag_x + mag_x_z)
    ) + resist * ((mag_x - mag_x_z) - (mag_z - prev[7]))
    return emf_z, emf_y


def row_rates(prev, here, after, residual, edges, edges_after):
    log_rho, vel_x, vel_y, vel_z, entropy, mag_x, mag_y, mag_z = here
    drift = vel_y + residual
    half_x = 0.5 * vel_x
    half_w = 0.5 * drift
    half_z = 0.5 * vel_z

    def moved_by(index):
        center = here[index]
        fore, back = after[index], prev[index]
        left, right = y_dn(center), y_up(center)
        under, over = z_dn(center), z_up(center)
        d_x, d_y, d_z = fore - back, right - left, over - under
        total = ((fore + back) + (left + right)) + (under + over)
        rate = viscous * total - (6.0 * viscous) * center
        rate = rate - (half_x * d_x + half_w * d_y + half_z * d_z)
        return rate, d_x, d_y, d_z, left

    rate_l, l_x, l_y, l_z, _ = moved_by(0)
    rate_vx, vx_x, _, _, _ = moved_by(1)
    rate_vy, _, vy_y, _, vy_left = moved_by(2)
    rate_vz, _, _, vz_z, vz_left = moved_by(3)
    rate_s, s_x, s_y, s_z, _ = moved_by(4)

    two_bx = mag_x + after[5]
    two_by = mag_y + y_up(mag_y)
    two_bz = mag_z + z_up(mag_z)
    two_bx_left = y_dn(two_bx)
    diff_y = after[6] - prev[6]
    diff_z = after[7] - prev[7]
    cur_x = (y_up(two_bz) - y_dn(two_bz)) - (z_up(two_by) - z_dn(two_by))
    cur_y = (z_up(two_bx) - z_dn(two_bx)) - (diff_z + z_up(diff_z))
    cur_z = (diff_y + y_up(diff_y)) - (y_up(two_bx) - two_bx_left)
    inverse = jnp.exp(-log_rho)
    eighth = 0.125 * inverse
    rate_l = rate_l - 0.5 * (vx_x + vy_y + vz_z)
    rate_vx = (
        rate_vx
        - (0.5 * sound_sq) * (l_x + s_x)
        + eighth * (cur_y * two_bz - cur_z * two_by)
        + (2.0 * rotation) * vel_y
    )
    rate_vy = (
        rate_vy
        - (0.5 * sound_sq) * (l_y + s_y)
        + eighth * (cur_z * two_bx - cur_x * two_bz)
        - ((2.0 - shear_rate) * rotation) * vel_x
    )
    rate_vz = (
        rate_vz
        - (0.5 * sound_sq) * (l_z + s_z)
        + eighth * (cur_x * two_by - cur_y * two_bx)
    )
    rate_s = rate_s + (resist * 0.0625) * inverse * (cur_x * cur_x + cur_y * cur_y + cur_z * cur_z)

    emf_z, emf_y = edges
    emf_z_after, emf_y_after = edges_after
    pair_w = drift + (vy_left + residual_left(residual))
    pair_z = vel_z + vz_left
    mag_z_y = y_dn(mag_z)
    mag_y_z = z_dn(mag_y)
    emf_x = 0.125 * (
        (pair_z + z_dn(pair_z)) * (mag_y + mag_y_z) - (pair_w + z_dn(pair_w)) * (mag_z + mag_z_y)
    ) + resist * ((mag_z - mag_z_y) - (mag_y - mag_y_z))
    rate_bx = (emf_z - y_up(emf_z)) + (z_up(emf_y) - emf_y)
    rate_by = (
        (emf_x - z_up(emf_x))
        + (emf_z_after - emf_z)
        - (0.25 * shear_rate * rotation) * (two_bx + two_bx_left)
    )
    rate_bz = (emf_y - emf_y_after) + (y_up(emf_x) - emf_x)
    return [rate_l, rate_vx, rate_vy, rate_vz, rate_s, rate_bx, rate_by, rate_bz]


def residual_left(residual):
    return residual


def two_sections(fields, depth, rows):
    wide = rows + 2 * DEPTH
    pitch = wide + 2
    strip_at = wide

    def kernel(residual, source, out, moved, first, drift_rows, ends):
        lane = lax.broadcasted_iota(jnp.int32, (depth, LANES), 1)

        def widen_strips(ref):
            for field in range(fields):
                even = ref[field, strip_at + 1]
                odd = ref[field, strip_at + 2]
                ref[field, strip_at] = pltpu.roll(odd, STRIP, 1)
                ref[field, strip_at + 3] = pltpu.roll(even, LANES - STRIP, 1)

        strip_drift = [jnp.zeros((depth, LANES), jnp.float32) for _ in range(2)]
        for row in range(wide):
            value = jnp.full((depth, LANES), residual[row], jnp.float32)
            drift_rows[row] = value
            strip_drift[row % 2] = jnp.where(lane // STRIP == row // 2, value, strip_drift[row % 2])
        drift_rows[strip_at] = pltpu.roll(strip_drift[1], STRIP, 1)
        drift_rows[strip_at + 1] = strip_drift[0]
        drift_rows[strip_at + 2] = strip_drift[1]
        drift_rows[strip_at + 3] = pltpu.roll(strip_drift[0], LANES - STRIP, 1)
        for field in range(fields):
            for row in range(pitch):
                moved[field, row if row < wide else row + 1] = source[
                    pl.ds(field * depth * pitch + row, depth, stride=pitch), :
                ]
        widen_strips(moved)

        def row_of(ref, row):
            return [ref[field, row] for field in range(fields)]

        def edges_of(ref, row):
            prev, here = row_of(ref, row - 1), row_of(ref, row)
            return radial_edges(
                prev, here, prev[2] + drift_rows[row - 1], here[2] + drift_rows[row]
            )

        def step(ref, row, edges):
            prev, here, after = row_of(ref, row - 1), row_of(ref, row), row_of(ref, row + 1)
            edges_after = radial_edges(
                here, after, here[2] + drift_rows[row], after[2] + drift_rows[row + 1]
            )
            rate = row_rates(prev, here, after, drift_rows[row], edges, edges_after)
            return [a + time_step * b for a, b in zip(here, rate)], edges_after

        def first_row(row, edges):
            result, edges = step(moved, row, edges)
            for field in range(fields):
                first[field, row] = result[field]
            return edges

        edges = edges_of(moved, strip_at + 1)
        for row in (strip_at + 1, strip_at + 2):
            edges = first_row(row, edges)
        widen_strips(first)
        lax.fori_loop(1, wide - 1, first_row, edges_of(moved, 1))

        edges = edges_of(first, strip_at + 1)
        for parity in range(2):
            result, edges = step(first, strip_at + 1 + parity, edges)
            for field in range(fields):
                ends[field, parity] = 0.5 * (moved[field, strip_at + 1 + parity] + result[field])

        def second_row(row, edges):
            result, edges = step(first, row, edges)
            place = row // 2
            turn = (LANES - 3 * DEPTH - STRIP * place) % LANES
            for field in range(fields):
                whole = 0.5 * (moved[field, row] + result[field])
                end = pltpu.roll(ends[field, row % 2], turn, 1)
                out[pl.ds(field * depth * rows + row - DEPTH, depth, stride=rows), :] = jnp.where(
                    lane < LANES - 2 * DEPTH, pltpu.roll(whole, LANES - DEPTH, 1), end
                )
            return edges

        lax.fori_loop(DEPTH, wide - DEPTH, second_row, edges_of(first, DEPTH))

    return pl.pallas_call(
        kernel,
        in_specs=[pl.BlockSpec(memory_space=pltpu.SMEM), pl.BlockSpec(memory_space=pltpu.VMEM)],
        out_shape=jax.ShapeDtypeStruct((fields * depth * rows, LANES), jnp.float32),
        out_specs=pl.BlockSpec(memory_space=pltpu.VMEM),
        scratch_shapes=[
            pltpu.VMEM((fields, wide + 4, depth, LANES), jnp.float32),
            pltpu.VMEM((fields, wide + 4, depth, LANES), jnp.float32),
            pltpu.VMEM((wide + 4, depth, LANES), jnp.float32),
            pltpu.VMEM((fields, 2, depth, LANES), jnp.float32),
        ],
        compiler_params=pltpu.CompilerParams(vmem_limit_bytes=24 * 1024 * 1024),
        name="two_sections",
    )


def local(state, residual, shift_rows, shear_offset):
    fields, depth, rows, cols = state.shape
    groups = lax.axis_size("gy")
    radial_count = lax.axis_size("gx")
    row_dev = lax.axis_index("gx")
    cells_y = cols * groups
    planes = fields * depth // groups
    offset = shear_offset[0]

    lines = lax.all_to_all(
        state.reshape(groups, planes, rows, cols), "gy", split_axis=0, concat_axis=0, tiled=True
    )
    low = passed_along(lines[:, :, rows - DEPTH :], "gx", 1)
    high = passed_along(lines[:, :, :DEPTH], "gx", -1)
    low_shift = passed_along(shift_rows[rows - DEPTH :], "gx", 1)
    high_shift = passed_along(shift_rows[:DEPTH], "gx", -1)
    shifts = jnp.concatenate(
        [
            low_shift - jnp.where(row_dev == 0, offset, 0),
            shift_rows,
            high_shift + jnp.where(row_dev == radial_count - 1, offset, 0),
        ]
    )
    shifts = (shifts + DEPTH) % cells_y
    chunk = turn_lines(groups, rows, planes)(
        shifts,
        lines.reshape(groups, planes * rows, cols),
        low.reshape(groups, planes * DEPTH, cols),
        high.reshape(groups, planes * DEPTH, cols),
    )
    wide = lax.all_to_all(
        chunk.reshape(groups, -1, cols), "gy", split_axis=0, concat_axis=0, tiled=True
    )
    padded = jnp.concatenate([residual[-DEPTH:], residual, residual[:DEPTH]])
    drift = lax.dynamic_slice_in_dim(padded, row_dev * rows, rows + 2 * DEPTH)
    evolved = two_sections(fields, depth, rows)(drift, wide.reshape(-1, cols))
    return evolved.reshape(state.shape)


def solution(mesh):
    return jax.shard_map(
        local,
        mesh=mesh,
        in_specs=(P(None, None, "gx", "gy"), P(), P("gx"), P()),
        out_specs=P(None, None, "gx", "gy"),
        check_vma=False,
    )
```

```python
import jax
import jax.numpy as jnp
from jax import lax
from jax.experimental import pallas as pl
from jax.experimental.pallas import tpu as pltpu
from jax.sharding import PartitionSpec as P

time_step = 0.2
viscous = 0.1
resist = 0.1
sound_sq = 1.0
rotation = 0.5
shear_rate = 1.5

LANES = 128
DEPTH = 2
STRIP = 4 * DEPTH


def passed_along(value, axis, steps):
    count = lax.axis_size(axis)
    pairs = [(source, (source + steps) % count) for source in range(count)]
    return lax.ppermute(value, axis, pairs)


def turn_lines(groups, rows, planes):
    own = rows * planes
    ghost = DEPTH * planes
    total = own + 2 * ghost
    wide = rows + 2 * DEPTH
    pitch = wide + 2

    def kernel(shifts, mine, low, high, out, lines, sems):
        copies = []
        for part, (source, start, size) in enumerate(
            ((mine, 0, own), (low, own, ghost), (high, own + ghost, ghost))
        ):
            for turn, (first, count, target) in enumerate(
                ((0, groups, 1), (0, groups, groups + 1), (groups - 1, 1, 0))
            ):
                copies.append(
                    pltpu.make_async_copy(
                        source.at[pl.ds(first, count)],
                        lines.at[pl.ds(target, count), pl.ds(start, size)],
                        sems.at[part, turn],
                    )
                )
        for copy in copies:
            copy.start()
        for copy in copies:
            copy.wait()
        flat = lines.reshape((2 * groups + 1) * total, LANES)
        lane = lax.broadcasted_iota(jnp.int32, (groups, LANES), 1)
        strips = [[jnp.zeros((groups, LANES), jnp.float32) for _ in range(planes)] for _ in range(2)]
        for row in range(wide):
            amount = shifts[row]
            block = (groups - amount // LANES) % groups
            part = amount % LANES
            keep = lane < LANES - part
            edge = ((lane + part) & (LANES - 1)) < 2 * DEPTH
            place = row // 2
            strip_turn = (part + 2 * DEPTH + STRIP * place) % LANES
            in_place = (lane >= STRIP * place) & (lane < STRIP * (place + 1))
            for plane in range(planes):
                if row < DEPTH:
                    line = own + plane * DEPTH + row
                elif row < DEPTH + rows:
                    line = plane * rows + row - DEPTH
                else:
                    line = own + ghost + plane * DEPTH + row - DEPTH - rows
                before, here, after = (
                    flat[pl.ds((block + ahead_by) * total + line, groups, stride=total), :]
                    for ahead_by in range(3)
                )
                window = jnp.where(keep, here, before)
                out[pl.ds(plane * pitch + row, groups, stride=planes * pitch), :] = pltpu.roll(
                    window, part, 1
                )
                rim = jnp.where(edge, jnp.where(keep, after, here), window)
                strips[row % 2][plane] = jnp.where(
                    in_place, pltpu.roll(rim, strip_turn, 1), strips[row % 2][plane]
                )
        for parity in range(2):
            for plane in range(planes):
                out[pl.ds(plane * pitch + wide + parity, groups, stride=planes * pitch), :] = strips[
                    parity
                ][plane]

    return pl.pallas_call(
        kernel,
        in_specs=[pl.BlockSpec(memory_space=pltpu.SMEM)] + [pl.BlockSpec(memory_space=pl.ANY)] * 3,
        out_shape=jax.ShapeDtypeStruct((groups * planes * pitch, LANES), jnp.float32),
        out_specs=pl.BlockSpec(memory_space=pltpu.VMEM),
        scratch_shapes=[
            pltpu.VMEM((2 * groups + 1, total, LANES), jnp.float32),
            pltpu.SemaphoreType.DMA((3, 3)),
        ],
        compiler_params=pltpu.CompilerParams(vmem_limit_bytes=24 * 1024 * 1024),
        name="turn_lines",
    )


def y_up(tile):
    return pltpu.roll(tile, LANES - 1, 1)


def y_dn(tile):
    return pltpu.roll(tile, 1, 1)


def z_up(tile):
    return pltpu.roll(tile, tile.shape[0] - 1, 0)


def z_dn(tile):
    return pltpu.roll(tile, 1, 0)


def radial_edges(prev, here, drift_prev, drift):
    _, vel_x, _, vel_z, _, mag_x, mag_y, mag_z = here
    two_x = vel_x + prev[1]
    two_z = vel_z + prev[3]
    two_w = drift + drift_prev
    mag_x_y = y_dn(mag_x)
    mag_x_z = z_dn(mag_x)
    emf_z = 0.125 * (
        (two_w + y_dn(two_w)) * (mag_x + mag_x_y) - (two_x + y_dn(two_x)) * (mag_y + prev[6])
    ) + resist * ((mag_y - prev[6]) - (mag_x - mag_x_y))
    emf_y = 0.125 * (
        (two_x + z_dn(two_x)) * (mag_z + prev[7]) - (two_z + z_dn(two_z)) * (mag_x + mag_x_z)
    ) + resist * ((mag_x - mag_x_z) - (mag_z - prev[7]))
    return emf_z, emf_y


def row_rates(prev, here, after, residual, edges, edges_after):
    log_rho, vel_x, vel_y, vel_z, entropy, mag_x, mag_y, mag_z = here
    drift = vel_y + residual
    half_x = 0.5 * vel_x
    half_w = 0.5 * drift
    half_z = 0.5 * vel_z

    def moved_by(index):
        center = here[index]
        fore, back = after[index], prev[index]
        left, right = y_dn(center), y_up(center)
        under, over = z_dn(center), z_up(center)
        d_x, d_y, d_z = fore - back, right - left, over - under
        total = ((fore + back) + (left + right)) + (under + over)
        rate = viscous * total - (6.0 * viscous) * center
        rate = rate - (half_x * d_x + half_w * d_y + half_z * d_z)
        return rate, d_x, d_y, d_z, left

    rate_l, l_x, l_y, l_z, _ = moved_by(0)
    rate_vx, vx_x, _, _, _ = moved_by(1)
    rate_vy, _, vy_y, _, vy_left = moved_by(2)
    rate_vz, _, _, vz_z, vz_left = moved_by(3)
    rate_s, s_x, s_y, s_z, _ = moved_by(4)

    two_bx = mag_x + after[5]
    two_by = mag_y + y_up(mag_y)
    two_bz = mag_z + z_up(mag_z)
    two_bx_left = y_dn(two_bx)
    diff_y = after[6] - prev[6]
    diff_z = after[7] - prev[7]
    cur_x = (y_up(two_bz) - y_dn(two_bz)) - (z_up(two_by) - z_dn(two_by))
    cur_y = (z_up(two_bx) - z_dn(two_bx)) - (diff_z + z_up(diff_z))
    cur_z = (diff_y + y_up(diff_y)) - (y_up(two_bx) - two_bx_left)
    inverse = jnp.exp(-log_rho)
    eighth = 0.125 * inverse
    rate_l = rate_l - 0.5 * (vx_x + vy_y + vz_z)
    rate_vx = (
        rate_vx
        - (0.5 * sound_sq) * (l_x + s_x)
        + eighth * (cur_y * two_bz - cur_z * two_by)
        + (2.0 * rotation) * vel_y
    )
    rate_vy = (
        rate_vy
        - (0.5 * sound_sq) * (l_y + s_y)
        + eighth * (cur_z * two_bx - cur_x * two_bz)
        - ((2.0 - shear_rate) * rotation) * vel_x
    )
    rate_vz = (
        rate_vz
        - (0.5 * sound_sq) * (l_z + s_z)
        + eighth * (cur_x * two_by - cur_y * two_bx)
    )
    rate_s = rate_s + (resist * 0.0625) * inverse * (cur_x * cur_x + cur_y * cur_y + cur_z * cur_z)

    emf_z, emf_y = edges
    emf_z_after, emf_y_after = edges_after
    pair_w = drift + (vy_left + residual_left(residual))
    pair_z = vel_z + vz_left
    mag_z_y = y_dn(mag_z)
    mag_y_z = z_dn(mag_y)
    emf_x = 0.125 * (
        (pair_z + z_dn(pair_z)) * (mag_y + mag_y_z) - (pair_w + z_dn(pair_w)) * (mag_z + mag_z_y)
    ) + resist * ((mag_z - mag_z_y) - (mag_y - mag_y_z))
    rate_bx = (emf_z - y_up(emf_z)) + (z_up(emf_y) - emf_y)
    rate_by = (
        (emf_x - z_up(emf_x))
        + (emf_z_after - emf_z)
        - (0.25 * shear_rate * rotation) * (two_bx + two_bx_left)
    )
    rate_bz = (emf_y - emf_y_after) + (y_up(emf_x) - emf_x)
    return [rate_l, rate_vx, rate_vy, rate_vz, rate_s, rate_bx, rate_by, rate_bz]


def residual_left(residual):
    return residual


def two_sections(fields, depth, rows):
    wide = rows + 2 * DEPTH
    pitch = wide + 2
    strip_at = wide

    def kernel(residual, source, out, moved, first, drift_rows, ends):
        lane = lax.broadcasted_iota(jnp.int32, (depth, LANES), 1)

        def widen_strips(ref):
            for field in range(fields):
                even = ref[field, strip_at + 1]
                odd = ref[field, strip_at + 2]
                ref[field, strip_at] = pltpu.roll(odd, STRIP, 1)
                ref[field, strip_at + 3] = pltpu.roll(even, LANES - STRIP, 1)

        strip_drift = [jnp.zeros((depth, LANES), jnp.float32) for _ in range(2)]
        for row in range(wide):
            value = jnp.full((depth, LANES), residual[row], jnp.float32)
            drift_rows[row] = value
            strip_drift[row % 2] = jnp.where(lane // STRIP == row // 2, value, strip_drift[row % 2])
        drift_rows[strip_at] = pltpu.roll(strip_drift[1], STRIP, 1)
        drift_rows[strip_at + 1] = strip_drift[0]
        drift_rows[strip_at + 2] = strip_drift[1]
        drift_rows[strip_at + 3] = pltpu.roll(strip_drift[0], LANES - STRIP, 1)
        for field in range(fields):
            for row in range(pitch):
                moved[field, row if row < wide else row + 1] = source[
                    pl.ds(field * depth * pitch + row, depth, stride=pitch), :
                ]
        widen_strips(moved)

        def row_of(ref, row):
            return [ref[field, row] for field in range(fields)]

        def edges_of(ref, row):
            prev, here = row_of(ref, row - 1), row_of(ref, row)
            return radial_edges(
                prev, here, prev[2] + drift_rows[row - 1], here[2] + drift_rows[row]
            )

        def step(ref, row, edges):
            prev, here, after = row_of(ref, row - 1), row_of(ref, row), row_of(ref, row + 1)
            edges_after = radial_edges(
                here, after, here[2] + drift_rows[row], after[2] + drift_rows[row + 1]
            )
            rate = row_rates(prev, here, after, drift_rows[row], edges, edges_after)
            return [a + time_step * b for a, b in zip(here, rate)], edges_after

        def first_row(row, edges):
            result, edges = step(moved, row, edges)
            for field in range(fields):
                first[field, row] = result[field]
            return edges

        edges = edges_of(moved, strip_at + 1)
        for row in (strip_at + 1, strip_at + 2):
            edges = first_row(row, edges)
        widen_strips(first)
        lax.fori_loop(1, wide - 1, first_row, edges_of(moved, 1), unroll=3)

        edges = edges_of(first, strip_at + 1)
        for parity in range(2):
            result, edges = step(first, strip_at + 1 + parity, edges)
            for field in range(fields):
                ends[field, parity] = 0.5 * (moved[field, strip_at + 1 + parity] + result[field])

        def second_row(row, edges):
            result, edges = step(first, row, edges)
            place = row // 2
            turn = (LANES - 3 * DEPTH - STRIP * place) % LANES
            for field in range(fields):
                whole = 0.5 * (moved[field, row] + result[field])
                end = pltpu.roll(ends[field, row % 2], turn, 1)
                out[pl.ds(field * depth * rows + row - DEPTH, depth, stride=rows), :] = jnp.where(
                    lane < LANES - 2 * DEPTH, pltpu.roll(whole, LANES - DEPTH, 1), end
                )
            return edges

        lax.fori_loop(DEPTH, wide - DEPTH, second_row, edges_of(first, DEPTH), unroll=4)

    return pl.pallas_call(
        kernel,
        in_specs=[pl.BlockSpec(memory_space=pltpu.SMEM), pl.BlockSpec(memory_space=pltpu.VMEM)],
        out_shape=jax.ShapeDtypeStruct((fields * depth * rows, LANES), jnp.float32),
        out_specs=pl.BlockSpec(memory_space=pltpu.VMEM),
        scratch_shapes=[
            pltpu.VMEM((fields, wide + 4, depth, LANES), jnp.float32),
            pltpu.VMEM((fields, wide + 4, depth, LANES), jnp.float32),
            pltpu.VMEM((wide + 4, depth, LANES), jnp.float32),
            pltpu.VMEM((fields, 2, depth, LANES), jnp.float32),
        ],
        compiler_params=pltpu.CompilerParams(vmem_limit_bytes=24 * 1024 * 1024),
        name="two_sections",
    )


def local(state, residual, shift_rows, shear_offset):
    fields, depth, rows, cols = state.shape
    groups = lax.axis_size("gy")
    radial_count = lax.axis_size("gx")
    row_dev = lax.axis_index("gx")
    cells_y = cols * groups
    planes = fields * depth // groups
    offset = shear_offset[0]

    lines = lax.all_to_all(
        state.reshape(groups, planes, rows, cols), "gy", split_axis=0, concat_axis=0, tiled=True
    )
    low = passed_along(lines[:, :, rows - DEPTH :], "gx", 1)
    high = passed_along(lines[:, :, :DEPTH], "gx", -1)
    low_shift = passed_along(shift_rows[rows - DEPTH :], "gx", 1)
    high_shift = passed_along(shift_rows[:DEPTH], "gx", -1)
    shifts = jnp.concatenate(
        [
            low_shift - jnp.where(row_dev == 0, offset, 0),
            shift_rows,
            high_shift + jnp.where(row_dev == radial_count - 1, offset, 0),
        ]
    )
    shifts = (shifts + DEPTH) % cells_y
    chunk = turn_lines(groups, rows, planes)(
        shifts,
        lines.reshape(groups, planes * rows, cols),
        low.reshape(groups, planes * DEPTH, cols),
        high.reshape(groups, planes * DEPTH, cols),
    )
    wide = lax.all_to_all(
        chunk.reshape(groups, -1, cols), "gy", split_axis=0, concat_axis=0, tiled=True
    )
    padded = jnp.concatenate([residual[-DEPTH:], residual, residual[:DEPTH]])
    drift = lax.dynamic_slice_in_dim(padded, row_dev * rows, rows + 2 * DEPTH)
    evolved = two_sections(fields, depth, rows)(drift, wide.reshape(-1, cols))
    return evolved.reshape(state.shape)


def solution(mesh):
    return jax.shard_map(
        local,
        mesh=mesh,
        in_specs=(P(None, None, "gx", "gy"), P(), P("gx"), P()),
        out_specs=P(None, None, "gx", "gy"),
        check_vma=False,
    )
```

```python
import jax
import jax.numpy as jnp
from jax import lax
from jax.experimental import pallas as pl
from jax.experimental.pallas import tpu as pltpu
from jax.sharding import PartitionSpec as P

time_step = 0.2
viscous = 0.1
resist = 0.1
sound_sq = 1.0
rotation = 0.5
shear_rate = 1.5

LANES = 128
TILE_ROWS = 8
DEPTH = 2
STRIP = 4 * DEPTH


def passed_along(value, axis, steps):
    count = lax.axis_size(axis)
    pairs = [(source, (source + steps) % count) for source in range(count)]
    return lax.ppermute(value, axis, pairs)


def turned_line(flat, first_row, total, groups, amount, lane):
    block = (groups - amount // LANES) % groups
    part = amount % LANES
    keep = lane < LANES - part
    edge = ((lane + part) & (LANES - 1)) < 2 * DEPTH
    before, here, after = (
        flat[pl.ds((block + ahead_by) * total + first_row, groups, stride=total), :]
        for ahead_by in range(3)
    )
    window = jnp.where(keep, here, before)
    rim = jnp.where(edge, jnp.where(keep, after, here), window)
    return pltpu.roll(window, part, 1), rim, part


def placed_strip(rim, part, place, lane, strips):
    turn = (part + 2 * DEPTH + STRIP * place) % LANES
    in_place = (lane >= STRIP * place) & (lane < STRIP * (place + 1))
    return jnp.where(in_place, pltpu.roll(rim, turn, 1), strips)


def lay_twice(source, lines, start, size, groups):
    for block in range(groups):
        value = source[block]
        for target in (block + 1, block + 1 + groups):
            lines[target, pl.ds(start, size)] = value
        if block == groups - 1:
            lines[0, pl.ds(start, size)] = value


def turn_own(groups, rows, planes):
    own = rows * planes
    zone = planes * (2 * DEPTH + 2)

    def kernel(shifts, mine, out, strips_out, lines, windows, out_sem):
        lay_twice(mine, lines, 0, own, groups)
        flat = lines.reshape((2 * groups + 1) * own, LANES)
        target = windows.reshape(groups * own, LANES)
        lane = lax.broadcasted_iota(jnp.int32, (groups, LANES), 1)
        strips = [[jnp.zeros((groups, LANES), jnp.float32) for _ in range(planes)] for _ in range(2)]
        for row in range(rows):
            wide_row = row + DEPTH
            for plane in range(planes):
                line = plane * rows + row
                window, rim, part = turned_line(flat, line, own, groups, shifts[wide_row], lane)
                target[pl.ds(line, groups, stride=own), :] = window
                strips[wide_row % 2][plane] = placed_strip(
                    rim, part, wide_row // 2, lane, strips[wide_row % 2][plane]
                )
        for plane in range(planes):
            for parity in range(2):
                strips_out[plane * 2 + parity] = strips[parity][plane]
        leave = pltpu.make_async_copy(windows, out.at[:, pl.ds(0, own)], out_sem)
        leave.start()
        leave.wait()

    return pl.pallas_call(
        kernel,
        in_specs=[pl.BlockSpec(memory_space=pltpu.SMEM), pl.BlockSpec(memory_space=pltpu.VMEM)],
        out_shape=(
            jax.ShapeDtypeStruct((groups, own + zone, LANES), jnp.float32),
            jax.ShapeDtypeStruct((2 * planes, groups, LANES), jnp.float32),
        ),
        out_specs=(pl.BlockSpec(memory_space=pl.ANY), pl.BlockSpec(memory_space=pltpu.VMEM)),
        scratch_shapes=[
            pltpu.VMEM((2 * groups + 1, own, LANES), jnp.float32),
            pltpu.VMEM((groups, own, LANES), jnp.float32),
            pltpu.SemaphoreType.DMA,
        ],
        compiler_params=pltpu.CompilerParams(vmem_limit_bytes=24 * 1024 * 1024),
        cost_estimate=pl.CostEstimate(flops=4000000, bytes_accessed=4000000, transcendentals=0),
        name="turn_own",
    )


def turn_ghost(groups, rows, planes):
    own = rows * planes
    ghost = DEPTH * planes
    zone = 3 * ghost

    def kernel(shifts, low, high, strips_in, chunk, out, lines, windows, sems):
        lay_twice(low, lines, 0, ghost, groups)
        lay_twice(high, lines, ghost, ghost, groups)
        flat = lines.reshape((2 * groups + 1) * 2 * ghost, LANES)
        target = windows.reshape(3 * groups * ghost, LANES)
        lane = lax.broadcasted_iota(jnp.int32, (groups, LANES), 1)
        strips = [
            [strips_in[plane * 2 + parity] for plane in range(planes)] for parity in range(2)
        ]

        def leave(part):
            copy = pltpu.make_async_copy(
                windows.at[part], out.at[:, pl.ds(own + part * ghost, ghost)], sems.at[part]
            )
            copy.start()
            return copy

        copies = []
        for side in range(2):
            for row in range(DEPTH):
                wide_row = row + side * (rows + DEPTH)
                for plane in range(planes):
                    line = side * ghost + plane * DEPTH + row
                    window, rim, part = turned_line(
                        flat, line, 2 * ghost, groups, shifts[wide_row], lane
                    )
                    place = side * groups * ghost + plane * DEPTH + row
                    target[pl.ds(place, groups, stride=ghost), :] = window
                    strips[wide_row % 2][plane] = placed_strip(
                        rim, part, wide_row // 2, lane, strips[wide_row % 2][plane]
                    )
            copies.append(leave(side))
        for plane in range(planes):
            for parity in range(2):
                place = 2 * groups * ghost + plane * DEPTH + parity
                target[pl.ds(place, groups, stride=ghost), :] = strips[parity][plane]
        copies.append(leave(2))
        for copy in copies:
            copy.wait()

    return pl.pallas_call(
        kernel,
        in_specs=[pl.BlockSpec(memory_space=pltpu.SMEM)]
        + [pl.BlockSpec(memory_space=pltpu.VMEM)] * 3
        + [pl.BlockSpec(memory_space=pl.ANY)],
        out_shape=jax.ShapeDtypeStruct((groups, own + zone, LANES), jnp.float32),
        out_specs=pl.BlockSpec(memory_space=pl.ANY),
        input_output_aliases={4: 0},
        scratch_shapes=[
            pltpu.VMEM((2 * groups + 1, 2 * ghost, LANES), jnp.float32),
            pltpu.VMEM((3, groups, ghost, LANES), jnp.float32),
            pltpu.SemaphoreType.DMA((3,)),
        ],
        compiler_params=pltpu.CompilerParams(vmem_limit_bytes=24 * 1024 * 1024),
        name="turn_ghost",
    )


def y_up(tile):
    return pltpu.roll(tile, LANES - 1, 1)


def y_dn(tile):
    return pltpu.roll(tile, 1, 1)


def z_up(tile):
    return pltpu.roll(tile, tile.shape[0] - 1, 0)


def z_dn(tile):
    return pltpu.roll(tile, 1, 0)


def radial_edges(prev, here, drift_prev, drift):
    _, vel_x, _, vel_z, _, mag_x, mag_y, mag_z = here
    two_x = vel_x + prev[1]
    two_z = vel_z + prev[3]
    two_w = drift + drift_prev
    mag_x_y = y_dn(mag_x)
    mag_x_z = z_dn(mag_x)
    emf_z = 0.125 * (
        (two_w + y_dn(two_w)) * (mag_x + mag_x_y) - (two_x + y_dn(two_x)) * (mag_y + prev[6])
    ) + resist * ((mag_y - prev[6]) - (mag_x - mag_x_y))
    emf_y = 0.125 * (
        (two_x + z_dn(two_x)) * (mag_z + prev[7]) - (two_z + z_dn(two_z)) * (mag_x + mag_x_z)
    ) + resist * ((mag_x - mag_x_z) - (mag_z - prev[7]))
    return emf_z, emf_y


def row_rates(prev, here, after, residual, edges, edges_after):
    log_rho, vel_x, vel_y, vel_z, entropy, mag_x, mag_y, mag_z = here
    drift = vel_y + residual
    half_x = 0.5 * vel_x
    half_w = 0.5 * drift
    half_z = 0.5 * vel_z

    def moved_by(index):
        center = here[index]
        fore, back = after[index], prev[index]
        left, right = y_dn(center), y_up(center)
        under, over = z_dn(center), z_up(center)
        d_x, d_y, d_z = fore - back, right - left, over - under
        total = ((fore + back) + (left + right)) + (under + over)
        rate = viscous * total - (6.0 * viscous) * center
        rate = rate - (half_x * d_x + half_w * d_y + half_z * d_z)
        return rate, d_x, d_y, d_z, left

    rate_l, l_x, l_y, l_z, _ = moved_by(0)
    rate_vx, vx_x, _, _, _ = moved_by(1)
    rate_vy, _, vy_y, _, vy_left = moved_by(2)
    rate_vz, _, _, vz_z, vz_left = moved_by(3)
    rate_s, s_x, s_y, s_z, _ = moved_by(4)

    two_bx = mag_x + after[5]
    two_by = mag_y + y_up(mag_y)
    two_bz = mag_z + z_up(mag_z)
    two_bx_left = y_dn(two_bx)
    diff_y = after[6] - prev[6]
    diff_z = after[7] - prev[7]
    cur_x = (y_up(two_bz) - y_dn(two_bz)) - (z_up(two_by) - z_dn(two_by))
    cur_y = (z_up(two_bx) - z_dn(two_bx)) - (diff_z + z_up(diff_z))
    cur_z = (diff_y + y_up(diff_y)) - (y_up(two_bx) - two_bx_left)
    inverse = jnp.exp(-log_rho)
    eighth = 0.125 * inverse
    rate_l = rate_l - 0.5 * (vx_x + vy_y + vz_z)
    rate_vx = (
        rate_vx
        - (0.5 * sound_sq) * (l_x + s_x)
        + eighth * (cur_y * two_bz - cur_z * two_by)
        + (2.0 * rotation) * vel_y
    )
    rate_vy = (
        rate_vy
        - (0.5 * sound_sq) * (l_y + s_y)
        + eighth * (cur_z * two_bx - cur_x * two_bz)
        - ((2.0 - shear_rate) * rotation) * vel_x
    )
    rate_vz = (
        rate_vz
        - (0.5 * sound_sq) * (l_z + s_z)
        + eighth * (cur_x * two_by - cur_y * two_bx)
    )
    rate_s = rate_s + (resist * 0.0625) * inverse * (cur_x * cur_x + cur_y * cur_y + cur_z * cur_z)

    emf_z, emf_y = edges
    emf_z_after, emf_y_after = edges_after
    pair_w = drift + (vy_left + residual_left(residual))
    pair_z = vel_z + vz_left
    mag_z_y = y_dn(mag_z)
    mag_y_z = z_dn(mag_y)
    emf_x = 0.125 * (
        (pair_z + z_dn(pair_z)) * (mag_y + mag_y_z) - (pair_w + z_dn(pair_w)) * (mag_z + mag_z_y)
    ) + resist * ((mag_z - mag_z_y) - (mag_y - mag_y_z))
    rate_bx = (emf_z - y_up(emf_z)) + (z_up(emf_y) - emf_y)
    rate_by = (
        (emf_x - z_up(emf_x))
        + (emf_z_after - emf_z)
        - (0.25 * shear_rate * rotation) * (two_bx + two_bx_left)
    )
    rate_bz = (emf_y - emf_y_after) + (y_up(emf_x) - emf_x)
    return [rate_l, rate_vx, rate_vy, rate_vz, rate_s, rate_bx, rate_by, rate_bz]


def residual_left(residual):
    return residual


def two_sections(fields, depth, rows):
    wide = rows + 2 * DEPTH
    half = depth // 2
    own = half * rows
    ghost = half * DEPTH
    chunk = own + 3 * ghost
    strip_at = wide

    def kernel(residual, source, out, moved, first, drift_rows, ends, evolved, sems):
        flat_out = evolved.reshape(fields * depth * rows, LANES)
        lane = lax.broadcasted_iota(jnp.int32, (depth, LANES), 1)

        def widen_strips(ref):
            for field in range(fields):
                even = ref[field, strip_at + 1]
                odd = ref[field, strip_at + 2]
                ref[field, strip_at] = pltpu.roll(odd, STRIP, 1)
                ref[field, strip_at + 3] = pltpu.roll(even, LANES - STRIP, 1)

        strip_drift = [jnp.zeros((depth, LANES), jnp.float32) for _ in range(2)]
        for row in range(wide):
            value = jnp.full((depth, LANES), residual[row], jnp.float32)
            drift_rows[row] = value
            strip_drift[row % 2] = jnp.where(lane // STRIP == row // 2, value, strip_drift[row % 2])
        drift_rows[strip_at] = pltpu.roll(strip_drift[1], STRIP, 1)
        drift_rows[strip_at + 1] = strip_drift[0]
        drift_rows[strip_at + 2] = strip_drift[1]
        drift_rows[strip_at + 3] = pltpu.roll(strip_drift[0], LANES - STRIP, 1)
        under = lax.broadcasted_iota(jnp.int32, (depth, LANES), 0) < half

        def column(first, stride):
            return jnp.where(
                under,
                source[pl.ds(first, depth, stride=stride), :],
                source[pl.ds(first + chunk - half * stride, depth, stride=stride), :],
            )

        for field in range(fields):
            start = 2 * field * chunk
            for row in range(rows):
                moved[field, row + DEPTH] = column(start + row, rows)
            for entry in range(DEPTH):
                first_at = start + own + entry
                moved[field, entry] = column(first_at, DEPTH)
                moved[field, DEPTH + rows + entry] = column(first_at + ghost, DEPTH)
                moved[field, strip_at + 1 + entry] = column(first_at + 2 * ghost, DEPTH)
        widen_strips(moved)

        def row_of(ref, row):
            return [ref[field, row] for field in range(fields)]

        def edges_of(ref, row):
            prev, here = row_of(ref, row - 1), row_of(ref, row)
            return radial_edges(
                prev, here, prev[2] + drift_rows[row - 1], here[2] + drift_rows[row]
            )

        def step(ref, row, edges):
            prev, here, after = row_of(ref, row - 1), row_of(ref, row), row_of(ref, row + 1)
            edges_after = radial_edges(
                here, after, here[2] + drift_rows[row], after[2] + drift_rows[row + 1]
            )
            rate = row_rates(prev, here, after, drift_rows[row], edges, edges_after)
            return [a + time_step * b for a, b in zip(here, rate)], edges_after

        def first_row(row, edges):
            result, edges = step(moved, row, edges)
            for field in range(fields):
                first[field, row] = result[field]
            return edges

        edges = edges_of(moved, strip_at + 1)
        for row in (strip_at + 1, strip_at + 2):
            edges = first_row(row, edges)
        widen_strips(first)
        lax.fori_loop(1, wide - 1, first_row, edges_of(moved, 1), unroll=3)

        edges = edges_of(first, strip_at + 1)
        for parity in range(2):
            result, edges = step(first, strip_at + 1 + parity, edges)
            for field in range(fields):
                ends[field, parity] = 0.5 * (moved[field, strip_at + 1 + parity] + result[field])

        def second_row(row, edges):
            result, edges = step(first, row, edges)
            place = row // 2
            turn = (LANES - 3 * DEPTH - STRIP * place) % LANES
            for field in range(fields):
                whole = 0.5 * (moved[field, row] + result[field])
                end = pltpu.roll(ends[field, row % 2], turn, 1)
                flat_out[pl.ds(field * depth * rows + row - DEPTH, depth, stride=rows), :] = jnp.where(
                    lane < LANES - 2 * DEPTH, pltpu.roll(whole, LANES - DEPTH, 1), end
                )
            return edges

        edges = edges_of(first, DEPTH)
        copies = []
        for block in range(rows // TILE_ROWS):
            start = DEPTH + block * TILE_ROWS
            edges = lax.fori_loop(start, start + TILE_ROWS, second_row, edges, unroll=4)
            for field in range(fields):
                piece = (pl.ds(field * depth, depth), pl.ds(block * TILE_ROWS, TILE_ROWS))
                copy = pltpu.make_async_copy(evolved.at[piece], out.at[piece], sems.at[block, field])
                copy.start()
                copies.append(copy)
        for copy in copies:
            copy.wait()

    return pl.pallas_call(
        kernel,
        in_specs=[pl.BlockSpec(memory_space=pltpu.SMEM), pl.BlockSpec(memory_space=pltpu.VMEM)],
        out_shape=jax.ShapeDtypeStruct((fields * depth, rows, LANES), jnp.float32),
        out_specs=pl.BlockSpec(memory_space=pl.ANY),
        scratch_shapes=[
            pltpu.VMEM((fields, wide + 4, depth, LANES), jnp.float32),
            pltpu.VMEM((fields, wide + 4, depth, LANES), jnp.float32),
            pltpu.VMEM((wide + 4, depth, LANES), jnp.float32),
            pltpu.VMEM((fields, 2, depth, LANES), jnp.float32),
            pltpu.VMEM((fields * depth, rows, LANES), jnp.float32),
            pltpu.SemaphoreType.DMA((rows // TILE_ROWS, fields)),
        ],
        compiler_params=pltpu.CompilerParams(vmem_limit_bytes=24 * 1024 * 1024),
        name="two_sections",
    )


def local(state, residual, shift_rows, shear_offset):
    fields, depth, rows, cols = state.shape
    groups = lax.axis_size("gy")
    radial_count = lax.axis_size("gx")
    row_dev = lax.axis_index("gx")
    cells_y = cols * groups
    planes = fields * depth // groups
    offset = shear_offset[0]

    lines = lax.all_to_all(
        state.reshape(groups, planes, rows, cols), "gy", split_axis=0, concat_axis=0, tiled=True
    )
    low = passed_along(lines[:, :, rows - DEPTH :], "gx", 1)
    high = passed_along(lines[:, :, :DEPTH], "gx", -1)
    low_shift = passed_along(shift_rows[rows - DEPTH :], "gx", 1)
    high_shift = passed_along(shift_rows[:DEPTH], "gx", -1)
    shifts = jnp.concatenate(
        [
            low_shift - jnp.where(row_dev == 0, offset, 0),
            shift_rows,
            high_shift + jnp.where(row_dev == radial_count - 1, offset, 0),
        ]
    )
    shifts = (shifts + DEPTH) % cells_y
    own_shifts = jnp.concatenate([shift_rows[:DEPTH], shift_rows]) + DEPTH
    chunk, strips = turn_own(groups, rows, planes)(
        own_shifts % cells_y, lines.reshape(groups, planes * rows, cols)
    )
    chunk = turn_ghost(groups, rows, planes)(
        shifts,
        low.reshape(groups, planes * DEPTH, cols),
        high.reshape(groups, planes * DEPTH, cols),
        strips,
        chunk,
    )
    wide = lax.all_to_all(chunk, "gy", split_axis=0, concat_axis=0, tiled=True)
    padded = jnp.concatenate([residual[-DEPTH:], residual, residual[:DEPTH]])
    drift = lax.dynamic_slice_in_dim(padded, row_dev * rows, rows + 2 * DEPTH)
    evolved = two_sections(fields, depth, rows)(drift, wide.reshape(-1, cols))
    return evolved.reshape(state.shape)


def solution(mesh):
    return jax.shard_map(
        local,
        mesh=mesh,
        in_specs=(P(None, None, "gx", "gy"), P(), P("gx"), P()),
        out_specs=P(None, None, "gx", "gy"),
        check_vma=False,
    )
```

```python
import jax
import jax.numpy as jnp
from jax import lax
from jax.experimental import pallas as pl
from jax.experimental.pallas import tpu as pltpu
from jax.sharding import PartitionSpec as P

time_step = 0.2
viscous = 0.1
resist = 0.1
sound_sq = 1.0
rotation = 0.5
shear_rate = 1.5

LANES = 128
TILE_ROWS = 8
DEPTH = 2
STRIP = 4 * DEPTH


def passed_along(value, axis, steps):
    count = lax.axis_size(axis)
    pairs = [(source, (source + steps) % count) for source in range(count)]
    return lax.ppermute(value, axis, pairs)


def turned_line(flat, first_row, total, groups, amount, lane):
    block = (groups - amount // LANES) % groups
    part = amount % LANES
    keep = lane < LANES - part
    edge = ((lane + part) & (LANES - 1)) < 2 * DEPTH
    before, here, after = (
        flat[pl.ds((block + ahead_by) * total + first_row, groups, stride=total), :]
        for ahead_by in range(3)
    )
    window = jnp.where(keep, here, before)
    rim = jnp.where(edge, jnp.where(keep, after, here), window)
    return pltpu.roll(window, part, 1), rim, part


def placed_strip(rim, part, place, lane, strips):
    turn = (part + 2 * DEPTH + STRIP * place) % LANES
    in_place = (lane >= STRIP * place) & (lane < STRIP * (place + 1))
    return jnp.where(in_place, pltpu.roll(rim, turn, 1), strips)


def lay_twice(source, lines, start, size, groups):
    for block in range(groups):
        value = source[block]
        for target in (block + 1, block + 1 + groups):
            lines[target, pl.ds(start, size)] = value
        if block == groups - 1:
            lines[0, pl.ds(start, size)] = value


def turn_own(groups, rows, planes):
    own = rows * planes
    zone = planes * (2 * DEPTH + 2)

    def kernel(shifts, mine, out, strips_out, lines, windows, out_sem):
        lay_twice(mine, lines, 0, own, groups)
        flat = lines.reshape((2 * groups + 1) * own, LANES)
        target = windows.reshape(groups * own, LANES)
        lane = lax.broadcasted_iota(jnp.int32, (groups, LANES), 1)
        strips = [[jnp.zeros((groups, LANES), jnp.float32) for _ in range(planes)] for _ in range(2)]
        for row in range(rows):
            wide_row = row + DEPTH
            for plane in range(planes):
                line = plane * rows + row
                window, rim, part = turned_line(flat, line, own, groups, shifts[row], lane)
                target[pl.ds(line, groups, stride=own), :] = window
                strips[wide_row % 2][plane] = placed_strip(
                    rim, part, wide_row // 2, lane, strips[wide_row % 2][plane]
                )
        for plane in range(planes):
            for parity in range(2):
                strips_out[plane * 2 + parity] = strips[parity][plane]
        leave = pltpu.make_async_copy(windows, out.at[:, pl.ds(0, own)], out_sem)
        leave.start()
        leave.wait()

    return pl.pallas_call(
        kernel,
        in_specs=[pl.BlockSpec(memory_space=pltpu.SMEM), pl.BlockSpec(memory_space=pltpu.VMEM)],
        out_shape=(
            jax.ShapeDtypeStruct((groups, own + zone, LANES), jnp.float32),
            jax.ShapeDtypeStruct((2 * planes, groups, LANES), jnp.float32),
        ),
        out_specs=(pl.BlockSpec(memory_space=pl.ANY), pl.BlockSpec(memory_space=pltpu.VMEM)),
        scratch_shapes=[
            pltpu.VMEM((2 * groups + 1, own, LANES), jnp.float32),
            pltpu.VMEM((groups, own, LANES), jnp.float32),
            pltpu.SemaphoreType.DMA,
        ],
        compiler_params=pltpu.CompilerParams(vmem_limit_bytes=24 * 1024 * 1024),
        cost_estimate=pl.CostEstimate(flops=4000000, bytes_accessed=4000000, transcendentals=0),
        name="turn_own",
    )


def turn_ghost(groups, rows, planes):
    own = rows * planes
    ghost = DEPTH * planes
    zone = 3 * ghost

    def kernel(shift_tiles, low, high, strips_in, chunk, out, lines, windows, sems):
        amounts = [jnp.max(shift_tiles[entry]) for entry in range(2 * DEPTH)]
        lay_twice(low, lines, 0, ghost, groups)
        lay_twice(high, lines, ghost, ghost, groups)
        flat = lines.reshape((2 * groups + 1) * 2 * ghost, LANES)
        target = windows.reshape(3 * groups * ghost, LANES)
        lane = lax.broadcasted_iota(jnp.int32, (groups, LANES), 1)
        strips = [
            [strips_in[plane * 2 + parity] for plane in range(planes)] for parity in range(2)
        ]

        def leave(part):
            copy = pltpu.make_async_copy(
                windows.at[part], out.at[:, pl.ds(own + part * ghost, ghost)], sems.at[part]
            )
            copy.start()
            return copy

        copies = []
        for side in range(2):
            for row in range(DEPTH):
                wide_row = row + side * (rows + DEPTH)
                for plane in range(planes):
                    line = side * ghost + plane * DEPTH + row
                    window, rim, part = turned_line(
                        flat, line, 2 * ghost, groups, amounts[side * DEPTH + row], lane
                    )
                    place = side * groups * ghost + plane * DEPTH + row
                    target[pl.ds(place, groups, stride=ghost), :] = window
                    strips[wide_row % 2][plane] = placed_strip(
                        rim, part, wide_row // 2, lane, strips[wide_row % 2][plane]
                    )
            copies.append(leave(side))
        for plane in range(planes):
            for parity in range(2):
                place = 2 * groups * ghost + plane * DEPTH + parity
                target[pl.ds(place, groups, stride=ghost), :] = strips[parity][plane]
        copies.append(leave(2))
        for copy in copies:
            copy.wait()

    return pl.pallas_call(
        kernel,
        in_specs=[pl.BlockSpec(memory_space=pltpu.VMEM)] * 4
        + [pl.BlockSpec(memory_space=pl.ANY)],
        out_shape=jax.ShapeDtypeStruct((groups, own + zone, LANES), jnp.float32),
        out_specs=pl.BlockSpec(memory_space=pl.ANY),
        input_output_aliases={4: 0},
        scratch_shapes=[
            pltpu.VMEM((2 * groups + 1, 2 * ghost, LANES), jnp.float32),
            pltpu.VMEM((3, groups, ghost, LANES), jnp.float32),
            pltpu.SemaphoreType.DMA((3,)),
        ],
        compiler_params=pltpu.CompilerParams(vmem_limit_bytes=24 * 1024 * 1024),
        name="turn_ghost",
    )


def y_up(tile):
    return pltpu.roll(tile, LANES - 1, 1)


def y_dn(tile):
    return pltpu.roll(tile, 1, 1)


def z_up(tile):
    return pltpu.roll(tile, tile.shape[0] - 1, 0)


def z_dn(tile):
    return pltpu.roll(tile, 1, 0)


def low_side(here, residual):
    vel_y = y_dn(here[2])
    return y_dn(here[1]), vel_y + residual, y_dn(here[5]), vel_y


def radial_edges(prev, here, drift_prev, drift, low_prev, low):
    _, vel_x, _, vel_z, _, mag_x, mag_y, mag_z = here
    two_x = vel_x + prev[1]
    two_z = vel_z + prev[3]
    two_w = drift + drift_prev
    four_x = two_x + (low[0] + low_prev[0])
    four_w = two_w + (low[1] + low_prev[1])
    mag_x_z = z_dn(mag_x)
    emf_z = (0.125 * time_step) * (four_w * (mag_x + low[2]) - four_x * (mag_y + prev[6])) + (time_step * resist) * (
        (mag_y - prev[6]) - (mag_x - low[2])
    )
    emf_y = (0.125 * time_step) * (
        (two_x + z_dn(two_x)) * (mag_z + prev[7]) - (two_z + z_dn(two_z)) * (mag_x + mag_x_z)
    ) + (time_step * resist) * ((mag_x - mag_x_z) - (mag_z - prev[7]))
    return emf_z, emf_y


def row_step(prev, here, after, residual, low, low_after, edges, edges_after):
    log_rho, vel_x, vel_y, vel_z, entropy, mag_x, mag_y, mag_z = here
    drift = vel_y + residual
    half_x = (0.5 * time_step) * vel_x
    half_w = (0.5 * time_step) * drift
    half_z = (0.5 * time_step) * vel_z

    def moved_by(index, left=None):
        center = here[index]
        fore, back = after[index], prev[index]
        left = y_dn(center) if left is None else left
        right = y_up(center)
        under, over = z_dn(center), z_up(center)
        d_x, d_y, d_z = fore - back, right - left, over - under
        total = ((fore + back) + (left + right)) + (under + over)
        result = (time_step * viscous) * total + (1.0 - 6.0 * time_step * viscous) * center
        result = result - (half_x * d_x + half_w * d_y + half_z * d_z)
        return result, d_x, d_y, d_z, left

    next_l, l_x, l_y, l_z, _ = moved_by(0)
    next_vx, vx_x, _, _, _ = moved_by(1, low[0])
    next_vy, _, vy_y, _, _ = moved_by(2, low[3])
    next_vz, _, _, vz_z, vz_left = moved_by(3)
    next_s, s_x, s_y, s_z, _ = moved_by(4)

    two_bx = mag_x + after[5]
    two_by = mag_y + y_up(mag_y)
    two_bz = mag_z + z_up(mag_z)
    two_bx_left = low[2] + low_after[2]
    mag_z_y = y_dn(mag_z)
    diff_y = after[6] - prev[6]
    diff_z = after[7] - prev[7]
    cur_x = (y_up(two_bz) - (mag_z_y + z_up(mag_z_y))) - (z_up(two_by) - z_dn(two_by))
    cur_y = (z_up(two_bx) - z_dn(two_bx)) - (diff_z + z_up(diff_z))
    cur_z = (diff_y + two_bx_left) + y_up(diff_y - two_bx)
    inverse = jnp.exp(-log_rho)
    eighth = (0.125 * time_step) * inverse
    next_l = next_l - (0.5 * time_step) * (vx_x + vy_y + vz_z)
    next_vx = (
        next_vx
        - (0.5 * time_step * sound_sq) * (l_x + s_x)
        + eighth * (cur_y * two_bz - cur_z * two_by)
        + (2.0 * time_step * rotation) * vel_y
    )
    next_vy = (
        next_vy
        - (0.5 * time_step * sound_sq) * (l_y + s_y)
        + eighth * (cur_z * two_bx - cur_x * two_bz)
        - (time_step * (2.0 - shear_rate) * rotation) * vel_x
    )
    next_vz = (
        next_vz
        - (0.5 * time_step * sound_sq) * (l_z + s_z)
        + eighth * (cur_x * two_by - cur_y * two_bx)
    )
    next_s = next_s + (0.0625 * time_step * resist) * inverse * (cur_x * cur_x + cur_y * cur_y + cur_z * cur_z)

    emf_z, emf_y = edges
    emf_z_after, emf_y_after = edges_after
    pair_w = drift + low[1]
    pair_z = vel_z + vz_left
    mag_y_z = z_dn(mag_y)
    emf_x = (0.125 * time_step) * (
        (pair_z + z_dn(pair_z)) * (mag_y + mag_y_z) - (pair_w + z_dn(pair_w)) * (mag_z + mag_z_y)
    ) + (time_step * resist) * ((mag_z - mag_z_y) - (mag_y - mag_y_z))
    next_bx = mag_x + (emf_z - y_up(emf_z)) + (z_up(emf_y) - emf_y)
    next_by = (
        mag_y
        + (emf_x - z_up(emf_x))
        + (emf_z_after - emf_z)
        - (0.25 * time_step * shear_rate * rotation) * (two_bx + two_bx_left)
    )
    next_bz = mag_z + (emf_y - emf_y_after) + (y_up(emf_x) - emf_x)
    return [next_l, next_vx, next_vy, next_vz, next_s, next_bx, next_by, next_bz]


def drift_tiles(drift, depth):
    wide = drift.shape[0]
    pairs = jnp.broadcast_to(drift.reshape(wide // 2, 2, 1), (wide // 2, 2, STRIP))
    strips = jnp.pad(
        jnp.swapaxes(pairs, 0, 1).reshape(2, wide // 2 * STRIP),
        ((0, 0), (0, LANES - wide // 2 * STRIP)),
    )
    strips = jnp.stack(
        [jnp.roll(strips[1], STRIP), strips[0], strips[1], jnp.roll(strips[0], -STRIP)]
    )
    tiles = jnp.concatenate([jnp.broadcast_to(drift[:, None], (wide, LANES)), strips])
    return jnp.broadcast_to(tiles[:, None], (wide + 4, depth, LANES))


def two_sections(fields, depth, rows):
    wide = rows + 2 * DEPTH
    half = depth // 2
    own = half * rows
    ghost = half * DEPTH
    chunk = own + 3 * ghost
    strip_at = wide

    def kernel(drift_rows, source, out, moved, first, ends, evolved, sems):
        flat_out = evolved.reshape(fields * depth * rows, LANES)
        lane = lax.broadcasted_iota(jnp.int32, (depth, LANES), 1)

        def widen_strips(ref):
            for field in range(fields):
                even = ref[field, strip_at + 1]
                odd = ref[field, strip_at + 2]
                ref[field, strip_at] = pltpu.roll(odd, STRIP, 1)
                ref[field, strip_at + 3] = pltpu.roll(even, LANES - STRIP, 1)

        under = lax.broadcasted_iota(jnp.int32, (depth, LANES), 0) < half

        def column(first, stride):
            return jnp.where(
                under,
                source[pl.ds(first, depth, stride=stride), :],
                source[pl.ds(first + chunk - half * stride, depth, stride=stride), :],
            )

        for field in range(fields):
            start = 2 * field * chunk
            for row in range(rows):
                moved[field, row + DEPTH] = column(start + row, rows)
            for entry in range(DEPTH):
                first_at = start + own + entry
                moved[field, entry] = column(first_at, DEPTH)
                moved[field, DEPTH + rows + entry] = column(first_at + ghost, DEPTH)
                moved[field, strip_at + 1 + entry] = column(first_at + 2 * ghost, DEPTH)
        widen_strips(moved)

        def row_of(ref, row):
            return [ref[field, row] for field in range(fields)]

        def edges_of(ref, row):
            prev, here = row_of(ref, row - 1), row_of(ref, row)
            drift_prev, drift = prev[2] + drift_rows[row - 1], here[2] + drift_rows[row]
            low = low_side(here, drift_rows[row])
            low_prev = low_side(prev, drift_rows[row - 1])
            return low, radial_edges(prev, here, drift_prev, drift, low_prev, low)

        def step(ref, row, carried):
            low, edges = carried
            prev, here, after = row_of(ref, row - 1), row_of(ref, row), row_of(ref, row + 1)
            drift, drift_after = here[2] + drift_rows[row], after[2] + drift_rows[row + 1]
            low_after = low_side(after, drift_rows[row + 1])
            edges_after = radial_edges(here, after, drift, drift_after, low, low_after)
            result = row_step(
                prev, here, after, drift_rows[row], low, low_after, edges, edges_after
            )
            return result, (low_after, edges_after)

        def first_row(row, edges):
            result, edges = step(moved, row, edges)
            for field in range(fields):
                first[field, row] = result[field]
            return edges

        edges = edges_of(moved, strip_at + 1)
        for row in (strip_at + 1, strip_at + 2):
            edges = first_row(row, edges)
        widen_strips(first)
        lax.fori_loop(1, wide - 1, first_row, edges_of(moved, 1), unroll=6)

        edges = edges_of(first, strip_at + 1)
        for parity in range(2):
            result, edges = step(first, strip_at + 1 + parity, edges)
            for field in range(fields):
                ends[field, parity] = 0.5 * (moved[field, strip_at + 1 + parity] + result[field])

        def second_row(row, edges):
            result, edges = step(first, row, edges)
            place = row // 2
            turn = (LANES - 3 * DEPTH - STRIP * place) % LANES
            for field in range(fields):
                whole = 0.5 * (moved[field, row] + result[field])
                end = pltpu.roll(ends[field, row % 2], turn, 1)
                flat_out[pl.ds(field * depth * rows + row - DEPTH, depth, stride=rows), :] = jnp.where(
                    lane < LANES - 2 * DEPTH, pltpu.roll(whole, LANES - DEPTH, 1), end
                )
            return edges

        edges = edges_of(first, DEPTH)
        copies = []
        for block in range(rows // TILE_ROWS):
            start = DEPTH + block * TILE_ROWS
            edges = lax.fori_loop(start, start + TILE_ROWS, second_row, edges, unroll=4)
            for field in range(fields):
                piece = (pl.ds(field * depth, depth), pl.ds(block * TILE_ROWS, TILE_ROWS))
                copy = pltpu.make_async_copy(evolved.at[piece], out.at[piece], sems.at[block, field])
                copy.start()
                copies.append(copy)
        for copy in copies:
            copy.wait()

    return pl.pallas_call(
        kernel,
        in_specs=[pl.BlockSpec(memory_space=pltpu.VMEM), pl.BlockSpec(memory_space=pltpu.VMEM)],
        out_shape=jax.ShapeDtypeStruct((fields * depth, rows, LANES), jnp.float32),
        out_specs=pl.BlockSpec(memory_space=pl.ANY),
        scratch_shapes=[
            pltpu.VMEM((fields, wide + 4, depth, LANES), jnp.float32),
            pltpu.VMEM((fields, wide + 4, depth, LANES), jnp.float32),
            pltpu.VMEM((fields, 2, depth, LANES), jnp.float32),
            pltpu.VMEM((fields * depth, rows, LANES), jnp.float32),
            pltpu.SemaphoreType.DMA((rows // TILE_ROWS, fields)),
        ],
        compiler_params=pltpu.CompilerParams(vmem_limit_bytes=24 * 1024 * 1024),
        name="two_sections",
    )


def local(state, residual, shift_rows, shear_offset):
    fields, depth, rows, cols = state.shape
    groups = lax.axis_size("gy")
    radial_count = lax.axis_size("gx")
    row_dev = lax.axis_index("gx")
    cells_y = cols * groups
    planes = fields * depth // groups
    offset = shear_offset[0]

    lines = lax.all_to_all(
        state.reshape(groups, planes, rows, cols), "gy", split_axis=0, concat_axis=0, tiled=True
    )
    low = passed_along(lines[:, :, rows - DEPTH :], "gx", 1)
    high = passed_along(lines[:, :, :DEPTH], "gx", -1)
    low_shift = passed_along(shift_rows[rows - DEPTH :], "gx", 1)
    high_shift = passed_along(shift_rows[:DEPTH], "gx", -1)
    ghost_shifts = jnp.concatenate(
        [
            low_shift - jnp.where(row_dev == 0, offset, 0),
            high_shift + jnp.where(row_dev == radial_count - 1, offset, 0),
        ]
    )
    ghost_shifts = (ghost_shifts + DEPTH) % cells_y
    ghost_shifts = jnp.broadcast_to(ghost_shifts[:, None, None], (2 * DEPTH, TILE_ROWS, LANES))
    own_shifts = shift_rows + DEPTH
    chunk, strips = turn_own(groups, rows, planes)(
        own_shifts % cells_y, lines.reshape(groups, planes * rows, cols)
    )
    chunk = turn_ghost(groups, rows, planes)(
        ghost_shifts,
        low.reshape(groups, planes * DEPTH, cols),
        high.reshape(groups, planes * DEPTH, cols),
        strips,
        chunk,
    )
    wide = lax.all_to_all(chunk, "gy", split_axis=0, concat_axis=0, tiled=True)
    padded = jnp.concatenate([residual[-DEPTH:], residual, residual[:DEPTH]])
    drift = lax.dynamic_slice_in_dim(padded, row_dev * rows, rows + 2 * DEPTH)
    evolved = two_sections(fields, depth, rows)(
        drift_tiles(drift, depth), wide.reshape(-1, cols)
    )
    return evolved.reshape(state.shape)


def solution(mesh):
    return jax.shard_map(
        local,
        mesh=mesh,
        in_specs=(P(None, None, "gx", "gy"), P(), P("gx"), P()),
        out_specs=P(None, None, "gx", "gy"),
        check_vma=False,
    )
```

```python
import jax
import jax.numpy as jnp
from jax import lax
from jax.experimental import pallas as pl
from jax.experimental.pallas import tpu as pltpu
from jax.sharding import PartitionSpec as P

time_step = 0.2
viscous = 0.1
resist = 0.1
sound_sq = 1.0
rotation = 0.5
shear_rate = 1.5

LANES = 128
TILE_ROWS = 8
DEPTH = 2
STRIP = 4 * DEPTH


def passed_along(value, axis, steps):
    count = lax.axis_size(axis)
    pairs = [(source, (source + steps) % count) for source in range(count)]
    return lax.ppermute(value, axis, pairs)


def turned_line(flat, first_row, total, groups, amount, lane):
    block = (groups - amount // LANES) % groups
    part = amount % LANES
    keep = lane < LANES - part
    edge = ((lane + part) & (LANES - 1)) < 2 * DEPTH
    before, here, after = (
        flat[pl.ds((block + ahead_by) * total + first_row, groups, stride=total), :]
        for ahead_by in range(3)
    )
    window = jnp.where(keep, here, before)
    rim = jnp.where(edge, jnp.where(keep, after, here), window)
    return pltpu.roll(window, part, 1), rim, part


def placed_strip(rim, part, place, lane, strips):
    turn = (part + 2 * DEPTH + STRIP * place) % LANES
    in_place = (lane >= STRIP * place) & (lane < STRIP * (place + 1))
    return jnp.where(in_place, pltpu.roll(rim, turn, 1), strips)


def lay_twice(source, lines, start, size, groups):
    for block in range(groups):
        value = source[block]
        for target in (block + 1, block + 1 + groups):
            lines[target, pl.ds(start, size)] = value
        if block == groups - 1:
            lines[0, pl.ds(start, size)] = value


def turn_own(groups, rows, planes):
    own = rows * planes
    zone = planes * (2 * DEPTH + 2)

    def kernel(shifts, mine, out, strips_out, lines, windows, out_sem):
        lay_twice(mine, lines, 0, own, groups)
        flat = lines.reshape((2 * groups + 1) * own, LANES)
        target = windows.reshape(groups * own, LANES)
        lane = lax.broadcasted_iota(jnp.int32, (groups, LANES), 1)
        strips = [[jnp.zeros((groups, LANES), jnp.float32) for _ in range(planes)] for _ in range(2)]
        for row in range(rows):
            wide_row = row + DEPTH
            for plane in range(planes):
                line = plane * rows + row
                window, rim, part = turned_line(flat, line, own, groups, shifts[row], lane)
                target[pl.ds(line, groups, stride=own), :] = window
                strips[wide_row % 2][plane] = placed_strip(
                    rim, part, wide_row // 2, lane, strips[wide_row % 2][plane]
                )
        for plane in range(planes):
            for parity in range(2):
                strips_out[plane * 2 + parity] = strips[parity][plane]
        leave = pltpu.make_async_copy(windows, out.at[:, pl.ds(0, own)], out_sem)
        leave.start()
        leave.wait()

    return pl.pallas_call(
        kernel,
        in_specs=[pl.BlockSpec(memory_space=pltpu.SMEM), pl.BlockSpec(memory_space=pltpu.VMEM)],
        out_shape=(
            jax.ShapeDtypeStruct((groups, own + zone, LANES), jnp.float32),
            jax.ShapeDtypeStruct((2 * planes, groups, LANES), jnp.float32),
        ),
        out_specs=(pl.BlockSpec(memory_space=pl.ANY), pl.BlockSpec(memory_space=pltpu.VMEM)),
        scratch_shapes=[
            pltpu.VMEM((2 * groups + 1, own, LANES), jnp.float32),
            pltpu.VMEM((groups, own, LANES), jnp.float32),
            pltpu.SemaphoreType.DMA,
        ],
        compiler_params=pltpu.CompilerParams(vmem_limit_bytes=24 * 1024 * 1024),
        cost_estimate=pl.CostEstimate(flops=4000000, bytes_accessed=4000000, transcendentals=0),
        name="turn_own",
    )


def turn_ghost(groups, rows, planes):
    own = rows * planes
    ghost = DEPTH * planes
    zone = 3 * ghost

    def kernel(shift_tiles, low, high, strips_in, chunk, out, lines, windows, sems):
        shift_rows = shift_tiles[...]
        amounts = [shift_rows[entry, 0] for entry in range(2 * DEPTH)]
        lay_twice(low, lines, 0, ghost, groups)
        lay_twice(high, lines, ghost, ghost, groups)
        flat = lines.reshape((2 * groups + 1) * 2 * ghost, LANES)
        target = windows.reshape(3 * groups * ghost, LANES)
        lane = lax.broadcasted_iota(jnp.int32, (groups, LANES), 1)
        strips = [
            [strips_in[plane * 2 + parity] for plane in range(planes)] for parity in range(2)
        ]

        def leave(part):
            copy = pltpu.make_async_copy(
                windows.at[part], out.at[:, pl.ds(own + part * ghost, ghost)], sems.at[part]
            )
            copy.start()
            return copy

        copies = []
        for side in range(2):
            for row in range(DEPTH):
                wide_row = row + side * (rows + DEPTH)
                for plane in range(planes):
                    line = side * ghost + plane * DEPTH + row
                    window, rim, part = turned_line(
                        flat, line, 2 * ghost, groups, amounts[side * DEPTH + row], lane
                    )
                    place = side * groups * ghost + plane * DEPTH + row
                    target[pl.ds(place, groups, stride=ghost), :] = window
                    strips[wide_row % 2][plane] = placed_strip(
                        rim, part, wide_row // 2, lane, strips[wide_row % 2][plane]
                    )
            copies.append(leave(side))
        for plane in range(planes):
            for parity in range(2):
                place = 2 * groups * ghost + plane * DEPTH + parity
                target[pl.ds(place, groups, stride=ghost), :] = strips[parity][plane]
        copies.append(leave(2))
        for copy in copies:
            copy.wait()

    return pl.pallas_call(
        kernel,
        in_specs=[pl.BlockSpec(memory_space=pltpu.VMEM)] * 4
        + [pl.BlockSpec(memory_space=pl.ANY)],
        out_shape=jax.ShapeDtypeStruct((groups, own + zone, LANES), jnp.float32),
        out_specs=pl.BlockSpec(memory_space=pl.ANY),
        input_output_aliases={4: 0},
        scratch_shapes=[
            pltpu.VMEM((2 * groups + 1, 2 * ghost, LANES), jnp.float32),
            pltpu.VMEM((3, groups, ghost, LANES), jnp.float32),
            pltpu.SemaphoreType.DMA((3,)),
        ],
        compiler_params=pltpu.CompilerParams(vmem_limit_bytes=24 * 1024 * 1024),
        name="turn_ghost",
    )


def y_up(tile):
    return pltpu.roll(tile, LANES - 1, 1)


def y_dn(tile):
    return pltpu.roll(tile, 1, 1)


def z_up(tile):
    return pltpu.roll(tile, tile.shape[0] - 1, 0)


def z_dn(tile):
    return pltpu.roll(tile, 1, 0)


def low_side(here, residual):
    vel_y = y_dn(here[2])
    return y_dn(here[1]), vel_y + residual, y_dn(here[5]), vel_y


def radial_edges(prev, here, drift_prev, drift, low_prev, low):
    _, vel_x, _, vel_z, _, mag_x, mag_y, mag_z = here
    two_x = vel_x + prev[1]
    two_z = vel_z + prev[3]
    two_w = drift + drift_prev
    four_x = two_x + (low[0] + low_prev[0])
    four_w = two_w + (low[1] + low_prev[1])
    mag_x_z = z_dn(mag_x)
    emf_z = (0.125 * time_step) * (four_w * (mag_x + low[2]) - four_x * (mag_y + prev[6])) + (time_step * resist) * (
        (mag_y - prev[6]) - (mag_x - low[2])
    )
    emf_y = (0.125 * time_step) * (
        (two_x + z_dn(two_x)) * (mag_z + prev[7]) - (two_z + z_dn(two_z)) * (mag_x + mag_x_z)
    ) + (time_step * resist) * ((mag_x - mag_x_z) - (mag_z - prev[7]))
    return emf_z, emf_y


def row_step(prev, here, after, residual, low, low_after, edges, edges_after):
    log_rho, vel_x, vel_y, vel_z, entropy, mag_x, mag_y, mag_z = here
    drift = vel_y + residual
    half_x = (0.5 * time_step) * vel_x
    half_w = (0.5 * time_step) * drift
    half_z = (0.5 * time_step) * vel_z

    def moved_by(index, left=None):
        center = here[index]
        fore, back = after[index], prev[index]
        left = y_dn(center) if left is None else left
        right = y_up(center)
        under, over = z_dn(center), z_up(center)
        d_x, d_y, d_z = fore - back, right - left, over - under
        total = ((fore + back) + (left + right)) + (under + over)
        result = (time_step * viscous) * total + (1.0 - 6.0 * time_step * viscous) * center
        result = result - (half_x * d_x + half_w * d_y + half_z * d_z)
        return result, d_x, d_y, d_z, left

    next_l, l_x, l_y, l_z, _ = moved_by(0)
    next_vx, vx_x, _, _, _ = moved_by(1, low[0])
    next_vy, _, vy_y, _, _ = moved_by(2, low[3])
    next_vz, _, _, vz_z, vz_left = moved_by(3)
    next_s, s_x, s_y, s_z, _ = moved_by(4)

    two_bx = mag_x + after[5]
    two_by = mag_y + y_up(mag_y)
    two_bz = mag_z + z_up(mag_z)
    two_bx_left = low[2] + low_after[2]
    mag_z_y = y_dn(mag_z)
    diff_y = after[6] - prev[6]
    diff_z = after[7] - prev[7]
    cur_x = (y_up(two_bz) - (mag_z_y + z_up(mag_z_y))) - (z_up(two_by) - z_dn(two_by))
    cur_y = (z_up(two_bx) - z_dn(two_bx)) - (diff_z + z_up(diff_z))
    cur_z = (diff_y + two_bx_left) + y_up(diff_y - two_bx)
    inverse = jnp.exp(-log_rho)
    eighth = (0.125 * time_step) * inverse
    next_l = next_l - (0.5 * time_step) * (vx_x + vy_y + vz_z)
    next_vx = (
        next_vx
        - (0.5 * time_step * sound_sq) * (l_x + s_x)
        + eighth * (cur_y * two_bz - cur_z * two_by)
        + (2.0 * time_step * rotation) * vel_y
    )
    next_vy = (
        next_vy
        - (0.5 * time_step * sound_sq) * (l_y + s_y)
        + eighth * (cur_z * two_bx - cur_x * two_bz)
        - (time_step * (2.0 - shear_rate) * rotation) * vel_x
    )
    next_vz = (
        next_vz
        - (0.5 * time_step * sound_sq) * (l_z + s_z)
        + eighth * (cur_x * two_by - cur_y * two_bx)
    )
    next_s = next_s + (0.0625 * time_step * resist) * inverse * (cur_x * cur_x + cur_y * cur_y + cur_z * cur_z)

    emf_z, emf_y = edges
    emf_z_after, emf_y_after = edges_after
    pair_w = drift + low[1]
    pair_z = vel_z + vz_left
    mag_y_z = z_dn(mag_y)
    emf_x = (0.125 * time_step) * (
        (pair_z + z_dn(pair_z)) * (mag_y + mag_y_z) - (pair_w + z_dn(pair_w)) * (mag_z + mag_z_y)
    ) + (time_step * resist) * ((mag_z - mag_z_y) - (mag_y - mag_y_z))
    next_bx = mag_x + (emf_z - y_up(emf_z)) + (z_up(emf_y) - emf_y)
    next_by = (
        mag_y
        + (emf_x - z_up(emf_x))
        + (emf_z_after - emf_z)
        - (0.25 * time_step * shear_rate * rotation) * (two_bx + two_bx_left)
    )
    next_bz = mag_z + (emf_y - emf_y_after) + (y_up(emf_x) - emf_x)
    return [next_l, next_vx, next_vy, next_vz, next_s, next_bx, next_by, next_bz]


def drift_tiles(drift, depth):
    wide = drift.shape[0]
    pairs = jnp.broadcast_to(drift.reshape(wide // 2, 2, 1), (wide // 2, 2, STRIP))
    strips = jnp.pad(
        jnp.swapaxes(pairs, 0, 1).reshape(2, wide // 2 * STRIP),
        ((0, 0), (0, LANES - wide // 2 * STRIP)),
    )
    strips = jnp.stack(
        [jnp.roll(strips[1], STRIP), strips[0], strips[1], jnp.roll(strips[0], -STRIP)]
    )
    tiles = jnp.concatenate([jnp.broadcast_to(drift[:, None], (wide, LANES)), strips])
    return jnp.broadcast_to(tiles[:, None], (wide + 4, depth, LANES))


def two_sections(fields, depth, rows):
    wide = rows + 2 * DEPTH
    half = depth // 2
    own = half * rows
    ghost = half * DEPTH
    chunk = own + 3 * ghost
    strip_at = wide

    def kernel(drift_rows, source, out, moved, first, ends, evolved, sems):
        flat_out = evolved.reshape(fields * depth * rows, LANES)
        lane = lax.broadcasted_iota(jnp.int32, (depth, LANES), 1)

        def widen_strips(ref):
            for field in range(fields):
                even = ref[field, strip_at + 1]
                odd = ref[field, strip_at + 2]
                ref[field, strip_at] = pltpu.roll(odd, STRIP, 1)
                ref[field, strip_at + 3] = pltpu.roll(even, LANES - STRIP, 1)

        under = lax.broadcasted_iota(jnp.int32, (depth, LANES), 0) < half

        def column(first, stride):
            return jnp.where(
                under,
                source[pl.ds(first, depth, stride=stride), :],
                source[pl.ds(first + chunk - half * stride, depth, stride=stride), :],
            )

        for field in range(fields):
            start = 2 * field * chunk
            for row in range(rows):
                moved[field, row + DEPTH] = column(start + row, rows)
            for entry in range(DEPTH):
                first_at = start + own + entry
                moved[field, entry] = column(first_at, DEPTH)
                moved[field, DEPTH + rows + entry] = column(first_at + ghost, DEPTH)
                moved[field, strip_at + 1 + entry] = column(first_at + 2 * ghost, DEPTH)
        widen_strips(moved)

        def row_of(ref, row):
            return [ref[field, row] for field in range(fields)]

        def edges_of(ref, row):
            prev, here = row_of(ref, row - 1), row_of(ref, row)
            drift_prev, drift = prev[2] + drift_rows[row - 1], here[2] + drift_rows[row]
            low = low_side(here, drift_rows[row])
            low_prev = low_side(prev, drift_rows[row - 1])
            return low, radial_edges(prev, here, drift_prev, drift, low_prev, low)

        def step(ref, row, carried):
            low, edges = carried
            prev, here, after = row_of(ref, row - 1), row_of(ref, row), row_of(ref, row + 1)
            drift, drift_after = here[2] + drift_rows[row], after[2] + drift_rows[row + 1]
            low_after = low_side(after, drift_rows[row + 1])
            edges_after = radial_edges(here, after, drift, drift_after, low, low_after)
            result = row_step(
                prev, here, after, drift_rows[row], low, low_after, edges, edges_after
            )
            return result, (low_after, edges_after)

        def first_row(row, edges):
            result, edges = step(moved, row, edges)
            for field in range(fields):
                first[field, row] = result[field]
            return edges

        edges = edges_of(moved, strip_at + 1)
        for row in (strip_at + 1, strip_at + 2):
            edges = first_row(row, edges)
        widen_strips(first)
        lax.fori_loop(1, wide - 1, first_row, edges_of(moved, 1), unroll=6)

        edges = edges_of(first, strip_at + 1)
        for parity in range(2):
            result, edges = step(first, strip_at + 1 + parity, edges)
            for field in range(fields):
                ends[field, parity] = 0.5 * (moved[field, strip_at + 1 + parity] + result[field])

        def second_row(row, edges):
            result, edges = step(first, row, edges)
            place = row // 2
            turn = (LANES - 3 * DEPTH - STRIP * place) % LANES
            for field in range(fields):
                whole = 0.5 * (moved[field, row] + result[field])
                end = pltpu.roll(ends[field, row % 2], turn, 1)
                flat_out[pl.ds(field * depth * rows + row - DEPTH, depth, stride=rows), :] = jnp.where(
                    lane < LANES - 2 * DEPTH, pltpu.roll(whole, LANES - DEPTH, 1), end
                )
            return edges

        edges = edges_of(first, DEPTH)
        copies = []
        for block in range(rows // TILE_ROWS):
            start = DEPTH + block * TILE_ROWS
            edges = lax.fori_loop(start, start + TILE_ROWS, second_row, edges, unroll=4)
            for field in range(fields):
                piece = (pl.ds(field * depth, depth), pl.ds(block * TILE_ROWS, TILE_ROWS))
                copy = pltpu.make_async_copy(evolved.at[piece], out.at[piece], sems.at[block, field])
                copy.start()
                copies.append(copy)
        for copy in copies:
            copy.wait()

    return pl.pallas_call(
        kernel,
        in_specs=[pl.BlockSpec(memory_space=pltpu.VMEM), pl.BlockSpec(memory_space=pltpu.VMEM)],
        out_shape=jax.ShapeDtypeStruct((fields * depth, rows, LANES), jnp.float32),
        out_specs=pl.BlockSpec(memory_space=pl.ANY),
        scratch_shapes=[
            pltpu.VMEM((fields, wide + 4, depth, LANES), jnp.float32),
            pltpu.VMEM((fields, wide + 4, depth, LANES), jnp.float32),
            pltpu.VMEM((fields, 2, depth, LANES), jnp.float32),
            pltpu.VMEM((fields * depth, rows, LANES), jnp.float32),
            pltpu.SemaphoreType.DMA((rows // TILE_ROWS, fields)),
        ],
        compiler_params=pltpu.CompilerParams(vmem_limit_bytes=24 * 1024 * 1024),
        name="two_sections",
    )


def local(state, residual, shift_rows, shear_offset):
    fields, depth, rows, cols = state.shape
    groups = lax.axis_size("gy")
    radial_count = lax.axis_size("gx")
    row_dev = lax.axis_index("gx")
    cells_y = cols * groups
    planes = fields * depth // groups
    offset = shear_offset[0]

    lines = lax.all_to_all(
        state.reshape(groups, planes, rows, cols), "gy", split_axis=0, concat_axis=0, tiled=True
    )
    low = passed_along(lines[:, :, rows - DEPTH :], "gx", 1)
    high = passed_along(lines[:, :, :DEPTH], "gx", -1)
    low_shift = passed_along(shift_rows[rows - DEPTH :], "gx", 1)
    high_shift = passed_along(shift_rows[:DEPTH], "gx", -1)
    across = jnp.ones((1, cols), jnp.int32)
    ghost_shifts = jnp.concatenate(
        [
            (low_shift - jnp.where(row_dev == 0, offset, 0))[:, None] * across,
            (high_shift + jnp.where(row_dev == radial_count - 1, offset, 0))[:, None] * across,
        ]
    )
    ghost_shifts = (ghost_shifts + DEPTH) % cells_y
    own_shifts = shift_rows + DEPTH
    chunk, strips = turn_own(groups, rows, planes)(
        own_shifts % cells_y, lines.reshape(groups, planes * rows, cols)
    )
    chunk = turn_ghost(groups, rows, planes)(
        ghost_shifts,
        low.reshape(groups, planes * DEPTH, cols),
        high.reshape(groups, planes * DEPTH, cols),
        strips,
        chunk,
    )
    wide = lax.all_to_all(chunk, "gy", split_axis=0, concat_axis=0, tiled=True)
    padded = jnp.concatenate([residual[-DEPTH:], residual, residual[:DEPTH]])
    drift = lax.dynamic_slice_in_dim(padded, row_dev * rows, rows + 2 * DEPTH)
    evolved = two_sections(fields, depth, rows)(
        drift_tiles(drift, depth), wide.reshape(-1, cols)
    )
    return evolved.reshape(state.shape)


def solution(mesh):
    return jax.shard_map(
        local,
        mesh=mesh,
        in_specs=(P(None, None, "gx", "gy"), P(), P("gx"), P()),
        out_specs=P(None, None, "gx", "gy"),
        check_vma=False,
    )
```

```python
import jax
import jax.numpy as jnp
from jax import lax
from jax.experimental import pallas as pl
from jax.experimental.pallas import tpu as pltpu
from jax.sharding import PartitionSpec as P

time_step = 0.2
viscous = 0.1
resist = 0.1
sound_sq = 1.0
rotation = 0.5
shear_rate = 1.5

LANES = 128
TILE_ROWS = 8
DEPTH = 2
STRIP = 4 * DEPTH


def passed_along(value, axis, steps):
    count = lax.axis_size(axis)
    pairs = [(source, (source + steps) % count) for source in range(count)]
    return lax.ppermute(value, axis, pairs)


def turned_line(flat, first_row, total, groups, amount, lane):
    block = (groups - amount // LANES) % groups
    part = amount % LANES
    keep = lane < LANES - part
    edge = ((lane + part) & (LANES - 1)) < 2 * DEPTH
    before, here, after = (
        flat[pl.ds((block + ahead_by) * total + first_row, groups, stride=total), :]
        for ahead_by in range(3)
    )
    window = jnp.where(keep, here, before)
    rim = jnp.where(edge, jnp.where(keep, after, here), window)
    return pltpu.roll(window, part, 1), rim, part


def placed_strip(rim, part, place, lane, strips):
    turn = (part + 2 * DEPTH + STRIP * place) % LANES
    in_place = (lane >= STRIP * place) & (lane < STRIP * (place + 1))
    return jnp.where(in_place, pltpu.roll(rim, turn, 1), strips)


def lay_twice(source, lines, start, size, groups):
    for block in range(groups):
        value = source[block]
        for target in (block + 1, block + 1 + groups):
            lines[target, pl.ds(start, size)] = value
        if block == groups - 1:
            lines[0, pl.ds(start, size)] = value


def turn_own(groups, rows, planes):
    own = rows * planes
    zone = planes * (2 * DEPTH + 2)

    def kernel(shifts, mine, out, strips_out, lines, windows, out_sem):
        lay_twice(mine, lines, 0, own, groups)
        flat = lines.reshape((2 * groups + 1) * own, LANES)
        target = windows.reshape(groups * own, LANES)
        lane = lax.broadcasted_iota(jnp.int32, (groups, LANES), 1)
        strips = [[jnp.zeros((groups, LANES), jnp.float32) for _ in range(planes)] for _ in range(2)]
        for row in range(rows):
            wide_row = row + DEPTH
            for plane in range(planes):
                line = plane * rows + row
                window, rim, part = turned_line(flat, line, own, groups, shifts[row], lane)
                target[pl.ds(line, groups, stride=own), :] = window
                strips[wide_row % 2][plane] = placed_strip(
                    rim, part, wide_row // 2, lane, strips[wide_row % 2][plane]
                )
        for plane in range(planes):
            for parity in range(2):
                strips_out[plane * 2 + parity] = strips[parity][plane]
        leave = pltpu.make_async_copy(windows, out.at[:, pl.ds(0, own)], out_sem)
        leave.start()
        leave.wait()

    return pl.pallas_call(
        kernel,
        in_specs=[pl.BlockSpec(memory_space=pltpu.SMEM), pl.BlockSpec(memory_space=pltpu.VMEM)],
        out_shape=(
            jax.ShapeDtypeStruct((groups, own + zone, LANES), jnp.float32),
            jax.ShapeDtypeStruct((2 * planes, groups, LANES), jnp.float32),
        ),
        out_specs=(pl.BlockSpec(memory_space=pl.ANY), pl.BlockSpec(memory_space=pltpu.VMEM)),
        scratch_shapes=[
            pltpu.VMEM((2 * groups + 1, own, LANES), jnp.float32),
            pltpu.VMEM((groups, own, LANES), jnp.float32),
            pltpu.SemaphoreType.DMA,
        ],
        compiler_params=pltpu.CompilerParams(vmem_limit_bytes=24 * 1024 * 1024),
        cost_estimate=pl.CostEstimate(flops=4000000, bytes_accessed=4000000, transcendentals=0),
        name="turn_own",
    )


def turn_ghost(groups, rows, planes):
    own = rows * planes
    ghost = DEPTH * planes
    zone = 3 * ghost

    def kernel(shift_tiles, low, high, strips_in, chunk, out, lines, windows, sems):
        shift_rows = shift_tiles[...]
        amounts = [shift_rows[entry, 0] for entry in range(2 * DEPTH)]
        lay_twice(low, lines, 0, ghost, groups)
        lay_twice(high, lines, ghost, ghost, groups)
        flat = lines.reshape((2 * groups + 1) * 2 * ghost, LANES)
        target = windows.reshape(3 * groups * ghost, LANES)
        lane = lax.broadcasted_iota(jnp.int32, (groups, LANES), 1)
        strips = [
            [strips_in[plane * 2 + parity] for plane in range(planes)] for parity in range(2)
        ]

        def leave(part):
            copy = pltpu.make_async_copy(
                windows.at[part], out.at[:, pl.ds(own + part * ghost, ghost)], sems.at[part]
            )
            copy.start()
            return copy

        copies = []
        for side in range(2):
            for row in range(DEPTH):
                wide_row = row + side * (rows + DEPTH)
                for plane in range(planes):
                    line = side * ghost + plane * DEPTH + row
                    window, rim, part = turned_line(
                        flat, line, 2 * ghost, groups, amounts[side * DEPTH + row], lane
                    )
                    place = side * groups * ghost + plane * DEPTH + row
                    target[pl.ds(place, groups, stride=ghost), :] = window
                    strips[wide_row % 2][plane] = placed_strip(
                        rim, part, wide_row // 2, lane, strips[wide_row % 2][plane]
                    )
            copies.append(leave(side))
        for plane in range(planes):
            for parity in range(2):
                place = 2 * groups * ghost + plane * DEPTH + parity
                target[pl.ds(place, groups, stride=ghost), :] = strips[parity][plane]
        copies.append(leave(2))
        for copy in copies:
            copy.wait()

    return pl.pallas_call(
        kernel,
        in_specs=[pl.BlockSpec(memory_space=pltpu.VMEM)] * 4
        + [pl.BlockSpec(memory_space=pl.ANY)],
        out_shape=jax.ShapeDtypeStruct((groups, own + zone, LANES), jnp.float32),
        out_specs=pl.BlockSpec(memory_space=pl.ANY),
        input_output_aliases={4: 0},
        scratch_shapes=[
            pltpu.VMEM((2 * groups + 1, 2 * ghost, LANES), jnp.float32),
            pltpu.VMEM((3, groups, ghost, LANES), jnp.float32),
            pltpu.SemaphoreType.DMA((3,)),
        ],
        compiler_params=pltpu.CompilerParams(vmem_limit_bytes=24 * 1024 * 1024),
        name="turn_ghost",
    )


def y_up(tile):
    return pltpu.roll(tile, LANES - 1, 1)


def y_dn(tile):
    return pltpu.roll(tile, 1, 1)


def z_up(tile):
    return pltpu.roll(tile, tile.shape[0] - 1, 0)


def z_dn(tile):
    return pltpu.roll(tile, 1, 0)


def both_sides(row):
    return [y_dn(field) for field in row], [y_up(field) for field in row]


def radial_edges(prev, here, drift_prev, drift, left_prev, left):
    _, vel_x, _, vel_z, _, mag_x, mag_y, mag_z = here
    two_x = vel_x + prev[1]
    two_z = vel_z + prev[3]
    two_w = drift + drift_prev
    four_x = two_x + (left[1] + left_prev[1])
    four_w = two_w + ((left[2] + left_prev[2]) + ((drift - here[2]) + (drift_prev - prev[2])))
    mag_x_z = z_dn(mag_x)
    emf_z = (0.125 * time_step) * (four_w * (mag_x + left[5]) - four_x * (mag_y + prev[6])) + (time_step * resist) * (
        (mag_y - prev[6]) - (mag_x - left[5])
    )
    emf_y = (0.125 * time_step) * (
        (two_x + z_dn(two_x)) * (mag_z + prev[7]) - (two_z + z_dn(two_z)) * (mag_x + mag_x_z)
    ) + (time_step * resist) * ((mag_x - mag_x_z) - (mag_z - prev[7]))
    return emf_z, emf_y


def row_step(prev, here, after, residual, ahead_prev, sides, sides_after, edges, edges_after):
    left, right = sides
    left_after, right_after = sides_after
    log_rho, vel_x, vel_y, vel_z, entropy, mag_x, mag_y, mag_z = here
    drift = vel_y + residual
    half_x = (0.5 * time_step) * vel_x
    half_w = (0.5 * time_step) * drift
    half_z = (0.5 * time_step) * vel_z

    def moved_by(index):
        center = here[index]
        fore, back = after[index], prev[index]
        behind, ahead = left[index], right[index]
        under, over = z_dn(center), z_up(center)
        d_x, d_y, d_z = fore - back, ahead - behind, over - under
        total = ((fore + back) + (behind + ahead)) + (under + over)
        result = (time_step * viscous) * total + (1.0 - 6.0 * time_step * viscous) * center
        result = result - (half_x * d_x + half_w * d_y + half_z * d_z)
        return result, d_x, d_y, d_z

    next_l, l_x, l_y, l_z = moved_by(0)
    next_vx, vx_x, _, _ = moved_by(1)
    next_vy, _, vy_y, _ = moved_by(2)
    next_vz, _, _, vz_z = moved_by(3)
    next_s, s_x, s_y, s_z = moved_by(4)

    two_bx = mag_x + after[5]
    two_by = mag_y + right[6]
    two_bz = mag_z + z_up(mag_z)
    two_bx_left = left[5] + left_after[5]
    mag_z_y = left[7]
    diff_y = after[6] - prev[6]
    diff_z = after[7] - prev[7]
    side_z = right[7] - mag_z_y
    cur_x = (side_z + z_up(side_z)) - (z_up(two_by) - z_dn(two_by))
    cur_y = (z_up(two_bx) - z_dn(two_bx)) - (diff_z + z_up(diff_z))
    cur_z = (diff_y + two_bx_left) + (
        (right_after[6] - ahead_prev) - (right[5] + right_after[5])
    )
    inverse = jnp.exp(-log_rho)
    eighth = (0.125 * time_step) * inverse
    next_l = next_l - (0.5 * time_step) * (vx_x + vy_y + vz_z)
    next_vx = (
        next_vx
        - (0.5 * time_step * sound_sq) * (l_x + s_x)
        + eighth * (cur_y * two_bz - cur_z * two_by)
        + (2.0 * time_step * rotation) * vel_y
    )
    next_vy = (
        next_vy
        - (0.5 * time_step * sound_sq) * (l_y + s_y)
        + eighth * (cur_z * two_bx - cur_x * two_bz)
        - (time_step * (2.0 - shear_rate) * rotation) * vel_x
    )
    next_vz = (
        next_vz
        - (0.5 * time_step * sound_sq) * (l_z + s_z)
        + eighth * (cur_x * two_by - cur_y * two_bx)
    )
    next_s = next_s + (0.0625 * time_step * resist) * inverse * (cur_x * cur_x + cur_y * cur_y + cur_z * cur_z)

    emf_z, emf_y = edges
    emf_z_after, emf_y_after = edges_after
    pair_w = (drift + residual) + left[2]
    pair_z = vel_z + left[3]
    mag_y_z = z_dn(mag_y)
    emf_x = (0.125 * time_step) * (
        (pair_z + z_dn(pair_z)) * (mag_y + mag_y_z) - (pair_w + z_dn(pair_w)) * (mag_z + mag_z_y)
    ) + (time_step * resist) * ((mag_z - mag_z_y) - (mag_y - mag_y_z))
    next_bx = (mag_x + emf_z) + (z_up(emf_y) - emf_y)
    next_by = (
        mag_y
        + (emf_x - z_up(emf_x))
        + (emf_z_after - emf_z)
        - (0.25 * time_step * shear_rate * rotation) * (two_bx + two_bx_left)
    )
    next_bz = (mag_z - emf_x) + (emf_y - emf_y_after)
    done = [next_l, next_vx, next_vy, next_vz, next_s, next_by]
    return done, (next_bx, emf_z, next_bz, emf_x)


DONE = (0, 1, 2, 3, 4, 6)


def last_edges(pending):
    next_bx, emf_z, next_bz, emf_x = pending
    return next_bx - y_up(emf_z), next_bz + y_up(emf_x)


def drift_tiles(drift, depth):
    wide = drift.shape[0]
    pairs = jnp.broadcast_to(drift.reshape(wide // 2, 2, 1), (wide // 2, 2, STRIP))
    strips = jnp.pad(
        jnp.swapaxes(pairs, 0, 1).reshape(2, wide // 2 * STRIP),
        ((0, 0), (0, LANES - wide // 2 * STRIP)),
    )
    strips = jnp.stack(
        [jnp.roll(strips[1], STRIP), strips[0], strips[1], jnp.roll(strips[0], -STRIP)]
    )
    tiles = jnp.concatenate([jnp.broadcast_to(drift[:, None], (wide, LANES)), strips])
    return jnp.broadcast_to(tiles[:, None], (wide + 4, depth, LANES))


def two_sections(fields, depth, rows):
    wide = rows + 2 * DEPTH
    half = depth // 2
    own = half * rows
    ghost = half * DEPTH
    chunk = own + 3 * ghost
    strip_at = wide

    def kernel(drift_rows, source, out, moved, first, whole, evolved, sems):
        flat_out = evolved.reshape(fields * depth * rows, LANES)
        lane = lax.broadcasted_iota(jnp.int32, (depth, LANES), 1)

        def widen_strips(ref):
            for field in range(fields):
                even = ref[field, strip_at + 1]
                odd = ref[field, strip_at + 2]
                ref[field, strip_at] = pltpu.roll(odd, STRIP, 1)
                ref[field, strip_at + 3] = pltpu.roll(even, LANES - STRIP, 1)

        under = lax.broadcasted_iota(jnp.int32, (depth, LANES), 0) < half

        def column(first, stride):
            return jnp.where(
                under,
                source[pl.ds(first, depth, stride=stride), :],
                source[pl.ds(first + chunk - half * stride, depth, stride=stride), :],
            )

        for field in range(fields):
            start = 2 * field * chunk
            for row in range(rows):
                moved[field, row + DEPTH] = column(start + row, rows)
            for entry in range(DEPTH):
                first_at = start + own + entry
                moved[field, entry] = column(first_at, DEPTH)
                moved[field, DEPTH + rows + entry] = column(first_at + ghost, DEPTH)
                moved[field, strip_at + 1 + entry] = column(first_at + 2 * ghost, DEPTH)
        widen_strips(moved)

        def row_of(ref, row):
            return [ref[field, row] for field in range(fields)]

        def begin(ref, row):
            prev, here = row_of(ref, row - 1), row_of(ref, row)
            sides_prev, sides = both_sides(prev), both_sides(here)
            edges = radial_edges(
                prev,
                here,
                prev[2] + drift_rows[row - 1],
                here[2] + drift_rows[row],
                sides_prev[0],
                sides[0],
            )
            return sides_prev[1][6], sides, edges, (here[5], here[5], here[7], here[7])

        def step(ref, row, carried):
            ahead_prev, sides, edges, _ = carried
            prev, here, after = row_of(ref, row - 1), row_of(ref, row), row_of(ref, row + 1)
            drift, drift_after = here[2] + drift_rows[row], after[2] + drift_rows[row + 1]
            sides_after = both_sides(after)
            edges_after = radial_edges(here, after, drift, drift_after, sides[0], sides_after[0])
            done, pending = row_step(
                prev, here, after, drift_rows[row], ahead_prev, sides, sides_after, edges, edges_after
            )
            return done, (sides[1][6], sides_after, edges_after, pending)

        def settle_first(row, carried):
            first[5, row], first[7, row] = last_edges(carried[3])

        def first_row(row, carried):
            settle_first(row - 1, carried)
            done, carried = step(moved, row, carried)
            for field, value in zip(DONE, done):
                first[field, row] = value
            return carried

        carried = begin(moved, strip_at + 1)
        for row in (strip_at + 1, strip_at + 2):
            carried = first_row(row, carried)
        settle_first(strip_at + 2, carried)
        widen_strips(first)
        carried = lax.fori_loop(1, wide - 1, first_row, begin(moved, 1), unroll=wide - 2)
        settle_first(wide - 2, carried)

        def settle_second(row, carried):
            for field, value in zip((5, 7), last_edges(carried[3])):
                whole[field, row] = 0.5 * (moved[field, row] + value)

        def second_row(row, carried):
            settle_second(row - 1, carried)
            done, carried = step(first, row, carried)
            for field, value in zip(DONE, done):
                whole[field, row] = 0.5 * (moved[field, row] + value)
            return carried

        carried = begin(first, strip_at + 1)
        for row in (strip_at + 1, strip_at + 2):
            carried = second_row(row, carried)
        settle_second(strip_at + 2, carried)

        carried = begin(first, DEPTH)
        copies = []
        for block in range(rows // TILE_ROWS):
            start = DEPTH + block * TILE_ROWS
            carried = lax.fori_loop(start, start + TILE_ROWS, second_row, carried, unroll=TILE_ROWS)
            settle_second(start + TILE_ROWS - 1, carried)
            for field in range(fields):
                for row in range(start, start + TILE_ROWS):
                    turn = (LANES - 3 * DEPTH - STRIP * (row // 2)) % LANES
                    end = pltpu.roll(whole[field, strip_at + 1 + row % 2], turn, 1)
                    flat_out[pl.ds(field * depth * rows + row - DEPTH, depth, stride=rows), :] = (
                        jnp.where(
                            lane < LANES - 2 * DEPTH,
                            pltpu.roll(whole[field, row], LANES - DEPTH, 1),
                            end,
                        )
                    )
                piece = (pl.ds(field * depth, depth), pl.ds(block * TILE_ROWS, TILE_ROWS))
                copy = pltpu.make_async_copy(evolved.at[piece], out.at[piece], sems.at[block, field])
                copy.start()
                copies.append(copy)
        for copy in copies:
            copy.wait()

    return pl.pallas_call(
        kernel,
        in_specs=[pl.BlockSpec(memory_space=pltpu.VMEM), pl.BlockSpec(memory_space=pltpu.VMEM)],
        out_shape=jax.ShapeDtypeStruct((fields * depth, rows, LANES), jnp.float32),
        out_specs=pl.BlockSpec(memory_space=pl.ANY),
        scratch_shapes=[
            pltpu.VMEM((fields, wide + 4, depth, LANES), jnp.float32),
            pltpu.VMEM((fields, wide + 4, depth, LANES), jnp.float32),
            pltpu.VMEM((fields, wide + 4, depth, LANES), jnp.float32),
            pltpu.VMEM((fields * depth, rows, LANES), jnp.float32),
            pltpu.SemaphoreType.DMA((rows // TILE_ROWS, fields)),
        ],
        compiler_params=pltpu.CompilerParams(vmem_limit_bytes=24 * 1024 * 1024),
        name="two_sections",
    )


def local(state, residual, shift_rows, shear_offset):
    fields, depth, rows, cols = state.shape
    groups = lax.axis_size("gy")
    radial_count = lax.axis_size("gx")
    row_dev = lax.axis_index("gx")
    cells_y = cols * groups
    planes = fields * depth // groups
    offset = shear_offset[0]

    lines = lax.all_to_all(
        state.reshape(groups, planes, rows, cols), "gy", split_axis=0, concat_axis=0, tiled=True
    )
    low = passed_along(lines[:, :, rows - DEPTH :], "gx", 1)
    high = passed_along(lines[:, :, :DEPTH], "gx", -1)
    low_shift = passed_along(shift_rows[rows - DEPTH :], "gx", 1)
    high_shift = passed_along(shift_rows[:DEPTH], "gx", -1)
    across = jnp.ones((1, cols), jnp.int32)
    ghost_shifts = jnp.concatenate(
        [
            (low_shift - jnp.where(row_dev == 0, offset, 0))[:, None] * across,
            (high_shift + jnp.where(row_dev == radial_count - 1, offset, 0))[:, None] * across,
        ]
    )
    ghost_shifts = (ghost_shifts + DEPTH) % cells_y
    own_shifts = shift_rows + DEPTH
    chunk, strips = turn_own(groups, rows, planes)(
        own_shifts % cells_y, lines.reshape(groups, planes * rows, cols)
    )
    chunk = turn_ghost(groups, rows, planes)(
        ghost_shifts,
        low.reshape(groups, planes * DEPTH, cols),
        high.reshape(groups, planes * DEPTH, cols),
        strips,
        chunk,
    )
    wide = lax.all_to_all(chunk, "gy", split_axis=0, concat_axis=0, tiled=True)
    padded = jnp.concatenate([residual[-DEPTH:], residual, residual[:DEPTH]])
    drift = lax.dynamic_slice_in_dim(padded, row_dev * rows, rows + 2 * DEPTH)
    evolved = two_sections(fields, depth, rows)(
        drift_tiles(drift, depth), wide.reshape(-1, cols)
    )
    return evolved.reshape(state.shape)


def solution(mesh):
    return jax.shard_map(
        local,
        mesh=mesh,
        in_specs=(P(None, None, "gx", "gy"), P(), P("gx"), P()),
        out_specs=P(None, None, "gx", "gy"),
        check_vma=False,
    )
```

```python
import jax
import jax.numpy as jnp
from jax import lax
from jax.experimental import pallas as pl
from jax.experimental.pallas import tpu as pltpu
from jax.sharding import PartitionSpec as P

time_step = 0.2
viscous = 0.1
resist = 0.1
sound_sq = 1.0
rotation = 0.5
shear_rate = 1.5

LANES = 128
TILE_ROWS = 8
FIRST = 1
DEPTH = 2
STRIP = 4 * DEPTH


def passed_along(value, axis, steps):
    count = lax.axis_size(axis)
    pairs = [(source, (source + steps) % count) for source in range(count)]
    return lax.ppermute(value, axis, pairs)


def turned_line(flat, first_row, total, groups, amount, lane):
    block = (groups - amount // LANES) % groups
    part = amount % LANES
    keep = lane < LANES - part
    edge = ((lane + part) & (LANES - 1)) < 2 * DEPTH
    before, here, after = (
        flat[pl.ds((block + ahead_by) * total + first_row, groups, stride=total), :]
        for ahead_by in range(3)
    )
    window = jnp.where(keep, here, before)
    rim = jnp.where(edge, jnp.where(keep, after, here), window)
    return pltpu.roll(window, part, 1), rim, part


def placed_strip(rim, part, place, lane, strips):
    turn = (part + 2 * DEPTH + STRIP * place) % LANES
    in_place = (lane >= STRIP * place) & (lane < STRIP * (place + 1))
    return jnp.where(in_place, pltpu.roll(rim, turn, 1), strips)


def lay_twice(source, lines, start, size, groups):
    for block in range(groups):
        value = source[block]
        for target in (block + 1, block + 1 + groups):
            lines[target, pl.ds(start, size)] = value
        if block == groups - 1:
            lines[0, pl.ds(start, size)] = value


def turn_own(groups, rows, planes):
    own = rows * planes
    zone = planes * (2 * DEPTH + 2)

    def kernel(shifts, mine, out, strips_out, lines, windows, out_sem):
        lay_twice(mine, lines, 0, own, groups)
        flat = lines.reshape((2 * groups + 1) * own, LANES)
        target = windows.reshape(groups * own, LANES)
        lane = lax.broadcasted_iota(jnp.int32, (groups, LANES), 1)
        strips = [[jnp.zeros((groups, LANES), jnp.float32) for _ in range(planes)] for _ in range(2)]
        for row in range(rows):
            wide_row = row + DEPTH
            for plane in range(planes):
                line = plane * rows + row
                window, rim, part = turned_line(flat, line, own, groups, shifts[row], lane)
                target[pl.ds(line, groups, stride=own), :] = window
                strips[wide_row % 2][plane] = placed_strip(
                    rim, part, wide_row // 2, lane, strips[wide_row % 2][plane]
                )
        for plane in range(planes):
            for parity in range(2):
                strips_out[plane * 2 + parity] = strips[parity][plane]
        leave = pltpu.make_async_copy(windows, out.at[:, pl.ds(0, own)], out_sem)
        leave.start()
        leave.wait()

    return pl.pallas_call(
        kernel,
        in_specs=[pl.BlockSpec(memory_space=pltpu.SMEM), pl.BlockSpec(memory_space=pltpu.VMEM)],
        out_shape=(
            jax.ShapeDtypeStruct((groups, own + zone, LANES), jnp.float32),
            jax.ShapeDtypeStruct((2 * planes, groups, LANES), jnp.float32),
        ),
        out_specs=(pl.BlockSpec(memory_space=pl.ANY), pl.BlockSpec(memory_space=pltpu.VMEM)),
        scratch_shapes=[
            pltpu.VMEM((2 * groups + 1, own, LANES), jnp.float32),
            pltpu.VMEM((groups, own, LANES), jnp.float32),
            pltpu.SemaphoreType.DMA,
        ],
        compiler_params=pltpu.CompilerParams(vmem_limit_bytes=24 * 1024 * 1024),
        cost_estimate=pl.CostEstimate(flops=4000000, bytes_accessed=4000000, transcendentals=0),
        name="turn_own",
    )


def turn_ghost(groups, rows, planes, side, last):
    own = rows * planes
    ghost = DEPTH * planes

    def kernel(source, strips_in, chunk, out, *rest):
        if last:
            lines, windows, sems = rest
        else:
            strips_out, lines, windows, sems = rest
        shift_rows = source[groups]
        amounts = [shift_rows[entry, 0].astype(jnp.int32) for entry in range(DEPTH)]
        lay_twice(source, lines, 0, ghost, groups)
        flat = lines.reshape((2 * groups + 1) * ghost, LANES)
        target = windows.reshape(2 * groups * ghost, LANES)
        lane = lax.broadcasted_iota(jnp.int32, (groups, LANES), 1)
        strips = [
            [strips_in[plane * 2 + parity] for plane in range(planes)] for parity in range(2)
        ]

        def leave(slot, part):
            copy = pltpu.make_async_copy(
                windows.at[slot], out.at[:, pl.ds(own + part * ghost, ghost)], sems.at[slot]
            )
            copy.start()
            return copy

        for row in range(DEPTH):
            wide_row = row + side * (rows + DEPTH)
            for plane in range(planes):
                place = plane * DEPTH + row
                window, rim, part = turned_line(flat, place, ghost, groups, amounts[row], lane)
                target[pl.ds(place, groups, stride=ghost), :] = window
                strips[wide_row % 2][plane] = placed_strip(
                    rim, part, wide_row // 2, lane, strips[wide_row % 2][plane]
                )
        copies = [leave(0, side)]
        for plane in range(planes):
            for parity in range(2):
                if last:
                    place = groups * ghost + plane * DEPTH + parity
                    target[pl.ds(place, groups, stride=ghost), :] = strips[parity][plane]
                else:
                    strips_out[plane * 2 + parity] = strips[parity][plane]
        if last:
            copies.append(leave(1, 2))
        for copy in copies:
            copy.wait()

    chunk_shape = jax.ShapeDtypeStruct((groups, own + 3 * ghost, LANES), jnp.float32)
    strip_shape = jax.ShapeDtypeStruct((2 * planes, groups, LANES), jnp.float32)
    return pl.pallas_call(
        kernel,
        in_specs=[pl.BlockSpec(memory_space=pltpu.VMEM)] * 2
        + [pl.BlockSpec(memory_space=pl.ANY)],
        out_shape=(chunk_shape,) if last else (chunk_shape, strip_shape),
        out_specs=(pl.BlockSpec(memory_space=pl.ANY),)
        + (() if last else (pl.BlockSpec(memory_space=pltpu.VMEM),)),
        input_output_aliases={2: 0},
        scratch_shapes=[
            pltpu.VMEM((2 * groups + 1, ghost, LANES), jnp.float32),
            pltpu.VMEM((2, groups, ghost, LANES), jnp.float32),
            pltpu.SemaphoreType.DMA((2,)),
        ],
        compiler_params=pltpu.CompilerParams(vmem_limit_bytes=24 * 1024 * 1024),
        name="turn_last_side" if last else "turn_first_side",
    )


def y_up(tile):
    return pltpu.roll(tile, LANES - 1, 1)


def y_dn(tile):
    return pltpu.roll(tile, 1, 1)


def z_up(tile):
    return pltpu.roll(tile, tile.shape[0] - 1, 0)


def z_dn(tile):
    return pltpu.roll(tile, 1, 0)


def both_sides(row):
    return [y_dn(field) for field in row], [y_up(field) for field in row]


def radial_edges(prev, here, drift_prev, drift, left_prev, left):
    _, vel_x, _, vel_z, _, mag_x, mag_y, mag_z = here
    two_x = vel_x + prev[1]
    two_z = vel_z + prev[3]
    two_w = drift + drift_prev
    four_x = two_x + (left[1] + left_prev[1])
    four_w = two_w + ((left[2] + left_prev[2]) + ((drift - here[2]) + (drift_prev - prev[2])))
    mag_x_z = z_dn(mag_x)
    emf_z = (0.125 * time_step) * (four_w * (mag_x + left[5]) - four_x * (mag_y + prev[6])) + (time_step * resist) * (
        (mag_y - prev[6]) - (mag_x - left[5])
    )
    emf_y = (0.125 * time_step) * (
        (two_x + z_dn(two_x)) * (mag_z + prev[7]) - (two_z + z_dn(two_z)) * (mag_x + mag_x_z)
    ) + (time_step * resist) * ((mag_x - mag_x_z) - (mag_z - prev[7]))
    return emf_z, emf_y


def row_step(prev, here, after, residual, ahead_prev, sides, sides_after, edges, edges_after):
    left, right = sides
    left_after, right_after = sides_after
    log_rho, vel_x, vel_y, vel_z, entropy, mag_x, mag_y, mag_z = here
    drift = vel_y + residual
    half_x = (0.5 * time_step) * vel_x
    half_w = (0.5 * time_step) * drift
    half_z = (0.5 * time_step) * vel_z

    def moved_by(index):
        center = here[index]
        fore, back = after[index], prev[index]
        behind, ahead = left[index], right[index]
        under, over = z_dn(center), z_up(center)
        d_x, d_y, d_z = fore - back, ahead - behind, over - under
        total = ((fore + back) + (behind + ahead)) + (under + over)
        result = (time_step * viscous) * total + (1.0 - 6.0 * time_step * viscous) * center
        result = result - (half_x * d_x + half_w * d_y + half_z * d_z)
        return result, d_x, d_y, d_z

    next_l, l_x, l_y, l_z = moved_by(0)
    next_vx, vx_x, _, _ = moved_by(1)
    next_vy, _, vy_y, _ = moved_by(2)
    next_vz, _, _, vz_z = moved_by(3)
    next_s, s_x, s_y, s_z = moved_by(4)

    two_bx = mag_x + after[5]
    two_by = mag_y + right[6]
    two_bz = mag_z + z_up(mag_z)
    two_bx_left = left[5] + left_after[5]
    mag_z_y = left[7]
    diff_y = after[6] - prev[6]
    diff_z = after[7] - prev[7]
    side_z = right[7] - mag_z_y
    cur_x = (side_z + z_up(side_z)) - (z_up(two_by) - z_dn(two_by))
    cur_y = (z_up(two_bx) - z_dn(two_bx)) - (diff_z + z_up(diff_z))
    cur_z = (diff_y + two_bx_left) + (
        (right_after[6] - ahead_prev) - (right[5] + right_after[5])
    )
    inverse = jnp.exp(-log_rho)
    eighth = (0.125 * time_step) * inverse
    next_l = next_l - (0.5 * time_step) * (vx_x + vy_y + vz_z)
    next_vx = (
        next_vx
        - (0.5 * time_step * sound_sq) * (l_x + s_x)
        + eighth * (cur_y * two_bz - cur_z * two_by)
        + (2.0 * time_step * rotation) * vel_y
    )
    next_vy = (
        next_vy
        - (0.5 * time_step * sound_sq) * (l_y + s_y)
        + eighth * (cur_z * two_bx - cur_x * two_bz)
        - (time_step * (2.0 - shear_rate) * rotation) * vel_x
    )
    next_vz = (
        next_vz
        - (0.5 * time_step * sound_sq) * (l_z + s_z)
        + eighth * (cur_x * two_by - cur_y * two_bx)
    )
    next_s = next_s + (0.0625 * time_step * resist) * inverse * (cur_x * cur_x + cur_y * cur_y + cur_z * cur_z)

    emf_z, emf_y = edges
    emf_z_after, emf_y_after = edges_after
    pair_w = (drift + residual) + left[2]
    pair_z = vel_z + left[3]
    mag_y_z = z_dn(mag_y)
    emf_x = (0.125 * time_step) * (
        (pair_z + z_dn(pair_z)) * (mag_y + mag_y_z) - (pair_w + z_dn(pair_w)) * (mag_z + mag_z_y)
    ) + (time_step * resist) * ((mag_z - mag_z_y) - (mag_y - mag_y_z))
    next_bx = (mag_x + emf_z) + (z_up(emf_y) - emf_y)
    next_by = (
        mag_y
        + (emf_x - z_up(emf_x))
        + (emf_z_after - emf_z)
        - (0.25 * time_step * shear_rate * rotation) * (two_bx + two_bx_left)
    )
    next_bz = (mag_z - emf_x) + (emf_y - emf_y_after)
    done = [next_l, next_vx, next_vy, next_vz, next_s, next_by]
    return done, (next_bx, emf_z, next_bz, emf_x)


DONE = (0, 1, 2, 3, 4, 6)


def last_edges(pending):
    next_bx, emf_z, next_bz, emf_x = pending
    return next_bx - y_up(emf_z), next_bz + y_up(emf_x)


def drift_tiles(drift, depth):
    wide = drift.shape[0]
    pairs = jnp.broadcast_to(drift.reshape(wide // 2, 2, 1), (wide // 2, 2, STRIP))
    strips = jnp.pad(
        jnp.swapaxes(pairs, 0, 1).reshape(2, wide // 2 * STRIP),
        ((0, 0), (0, LANES - wide // 2 * STRIP)),
    )
    strips = jnp.stack(
        [jnp.roll(strips[1], STRIP), strips[0], strips[1], jnp.roll(strips[0], -STRIP)]
    )
    tiles = jnp.concatenate([jnp.broadcast_to(drift[:, None], (wide, LANES)), strips])
    return jnp.broadcast_to(tiles[:, None], (wide + 4, depth, LANES))


def two_sections(fields, depth, rows):
    wide = rows + 2 * DEPTH
    half = depth // 2
    own = half * rows
    ghost = half * DEPTH
    chunk = own + 3 * ghost
    strip_at = wide

    def kernel(drift_rows, source, out, moved, first, whole, evolved, sems):
        flat_out = evolved.reshape(fields * depth * rows, LANES)
        lane = lax.broadcasted_iota(jnp.int32, (depth, LANES), 1)

        def widen_strips(ref):
            for field in range(fields):
                even = ref[field, strip_at + 1]
                odd = ref[field, strip_at + 2]
                ref[field, strip_at] = pltpu.roll(odd, STRIP, 1)
                ref[field, strip_at + 3] = pltpu.roll(even, LANES - STRIP, 1)

        under = lax.broadcasted_iota(jnp.int32, (depth, LANES), 0) < half

        def column(first, stride):
            return jnp.where(
                under,
                source[pl.ds(first, depth, stride=stride), :],
                source[pl.ds(first + chunk - half * stride, depth, stride=stride), :],
            )

        for field in range(fields):
            start = 2 * field * chunk
            for row in range(rows):
                moved[field, row + DEPTH] = column(start + row, rows)
            for entry in range(DEPTH):
                first_at = start + own + entry
                moved[field, entry] = column(first_at, DEPTH)
                moved[field, DEPTH + rows + entry] = column(first_at + ghost, DEPTH)
                moved[field, strip_at + 1 + entry] = column(first_at + 2 * ghost, DEPTH)
        widen_strips(moved)

        def row_of(ref, row):
            return [ref[field, row] for field in range(fields)]

        def begin(ref, row):
            prev, here = row_of(ref, row - 1), row_of(ref, row)
            sides_prev, sides = both_sides(prev), both_sides(here)
            edges = radial_edges(
                prev,
                here,
                prev[2] + drift_rows[row - 1],
                here[2] + drift_rows[row],
                sides_prev[0],
                sides[0],
            )
            return sides_prev[1][6], sides, edges, (here[5], here[5], here[7], here[7])

        def step(ref, row, carried):
            ahead_prev, sides, edges, _ = carried
            prev, here, after = row_of(ref, row - 1), row_of(ref, row), row_of(ref, row + 1)
            drift, drift_after = here[2] + drift_rows[row], after[2] + drift_rows[row + 1]
            sides_after = both_sides(after)
            edges_after = radial_edges(here, after, drift, drift_after, sides[0], sides_after[0])
            done, pending = row_step(
                prev, here, after, drift_rows[row], ahead_prev, sides, sides_after, edges, edges_after
            )
            return done, (sides[1][6], sides_after, edges_after, pending)

        def settle_first(row, carried):
            first[5, row], first[7, row] = last_edges(carried[3])

        def first_row(row, carried):
            settle_first(row - 1, carried)
            done, carried = step(moved, row, carried)
            for field, value in zip(DONE, done):
                first[field, row] = value
            return carried

        carried = begin(moved, strip_at + 1)
        for row in (strip_at + 1, strip_at + 2):
            carried = first_row(row, carried)
        settle_first(strip_at + 2, carried)
        widen_strips(first)
        carried = lax.fori_loop(1, wide - 1, first_row, begin(moved, 1), unroll=wide - 2)
        settle_first(wide - 2, carried)

        def settle_second(row, carried):
            for field, value in zip((5, 7), last_edges(carried[3])):
                whole[field, row] = 0.5 * (moved[field, row] + value)

        def second_row(row, carried):
            settle_second(row - 1, carried)
            done, carried = step(first, row, carried)
            for field, value in zip(DONE, done):
                whole[field, row] = 0.5 * (moved[field, row] + value)
            return carried

        carried = begin(first, strip_at + 1)
        for row in (strip_at + 1, strip_at + 2):
            carried = second_row(row, carried)
        settle_second(strip_at + 2, carried)

        carried = begin(first, DEPTH)
        copies = []
        for block in range(rows // TILE_ROWS):
            start = DEPTH + block * TILE_ROWS
            carried = lax.fori_loop(start, start + TILE_ROWS, second_row, carried, unroll=TILE_ROWS)
            settle_second(start + TILE_ROWS - 1, carried)
            for field in range(fields):
                for row in range(start, start + TILE_ROWS):
                    turn = (LANES - 3 * DEPTH - STRIP * (row // 2)) % LANES
                    end = pltpu.roll(whole[field, strip_at + 1 + row % 2], turn, 1)
                    flat_out[pl.ds(field * depth * rows + row - DEPTH, depth, stride=rows), :] = (
                        jnp.where(
                            lane < LANES - 2 * DEPTH,
                            pltpu.roll(whole[field, row], LANES - DEPTH, 1),
                            end,
                        )
                    )
                piece = (pl.ds(field * depth, depth), pl.ds(block * TILE_ROWS, TILE_ROWS))
                copy = pltpu.make_async_copy(evolved.at[piece], out.at[piece], sems.at[block, field])
                copy.start()
                copies.append(copy)
        for copy in copies:
            copy.wait()

    return pl.pallas_call(
        kernel,
        in_specs=[pl.BlockSpec(memory_space=pltpu.VMEM), pl.BlockSpec(memory_space=pltpu.VMEM)],
        out_shape=jax.ShapeDtypeStruct((fields * depth, rows, LANES), jnp.float32),
        out_specs=pl.BlockSpec(memory_space=pl.ANY),
        scratch_shapes=[
            pltpu.VMEM((fields, wide + 4, depth, LANES), jnp.float32),
            pltpu.VMEM((fields, wide + 4, depth, LANES), jnp.float32),
            pltpu.VMEM((fields, wide + 4, depth, LANES), jnp.float32),
            pltpu.VMEM((fields * depth, rows, LANES), jnp.float32),
            pltpu.SemaphoreType.DMA((rows // TILE_ROWS, fields)),
        ],
        compiler_params=pltpu.CompilerParams(vmem_limit_bytes=24 * 1024 * 1024),
        name="two_sections",
    )


def local(state, residual, shift_rows, shear_offset):
    fields, depth, rows, cols = state.shape
    groups = lax.axis_size("gy")
    radial_count = lax.axis_size("gx")
    row_dev = lax.axis_index("gx")
    cells_y = cols * groups
    planes = fields * depth // groups
    offset = shear_offset[0]

    lines = lax.all_to_all(
        state.reshape(groups, planes, rows, cols), "gy", split_axis=0, concat_axis=0, tiled=True
    )

    def with_shifts(part, shifts):
        shifts = ((shifts + DEPTH) % cells_y).astype(jnp.float32)
        extra = jnp.broadcast_to(shifts[None, None, :, None], (1, planes, DEPTH, cols))
        return jnp.concatenate([part, extra])

    up = jnp.where(row_dev == radial_count - 1, offset, 0)
    down = jnp.where(row_dev == 0, offset, 0)
    low = with_shifts(lines[:, :, rows - DEPTH :], shift_rows[rows - DEPTH :] - up)
    high = with_shifts(lines[:, :, :DEPTH], shift_rows[:DEPTH] + down)
    low, high = passed_along(low, "gx", 1), passed_along(high, "gx", -1)
    own_shifts = shift_rows + DEPTH
    chunk, strips = turn_own(groups, rows, planes)(
        own_shifts % cells_y, lines.reshape(groups, planes * rows, cols)
    )
    sides = (
        low.reshape(groups + 1, planes * DEPTH, cols),
        high.reshape(groups + 1, planes * DEPTH, cols),
    )
    chunk, strips = turn_ghost(groups, rows, planes, FIRST, False)(
        sides[FIRST], strips, chunk
    )
    (chunk,) = turn_ghost(groups, rows, planes, 1 - FIRST, True)(
        sides[1 - FIRST], strips, chunk
    )
    wide = lax.all_to_all(chunk, "gy", split_axis=0, concat_axis=0, tiled=True)
    padded = jnp.concatenate([residual[-DEPTH:], residual, residual[:DEPTH]])
    drift = lax.dynamic_slice_in_dim(padded, row_dev * rows, rows + 2 * DEPTH)
    evolved = two_sections(fields, depth, rows)(
        drift_tiles(drift, depth), wide.reshape(-1, cols)
    )
    return evolved.reshape(state.shape)


def solution(mesh):
    return jax.shard_map(
        local,
        mesh=mesh,
        in_specs=(P(None, None, "gx", "gy"), P(), P("gx"), P()),
        out_specs=P(None, None, "gx", "gy"),
        check_vma=False,
    )
```

```python
import jax
import jax.numpy as jnp
from jax import lax
from jax.experimental import pallas as pl
from jax.experimental.pallas import tpu as pltpu
from jax.sharding import PartitionSpec as P

time_step = 0.2
viscous = 0.1
resist = 0.1
sound_sq = 1.0
rotation = 0.5
shear_rate = 1.5

LANES = 128
TILE_ROWS = 8
DEPTH = 2
STRIP = 4 * DEPTH


def passed_along(value, axis, steps):
    count = lax.axis_size(axis)
    pairs = [(source, (source + steps) % count) for source in range(count)]
    return lax.ppermute(value, axis, pairs)


def turned_line(flat, first_row, total, groups, amount, lane):
    block = (groups - amount // LANES) % groups
    part = amount % LANES
    keep = lane < LANES - part
    edge = ((lane + part) & (LANES - 1)) < 2 * DEPTH
    before, here, after = (
        flat[pl.ds((block + ahead_by) * total + first_row, groups, stride=total), :]
        for ahead_by in range(3)
    )
    window = jnp.where(keep, here, before)
    rim = jnp.where(edge, jnp.where(keep, after, here), window)
    return pltpu.roll(window, part, 1), rim, part


def placed_strip(rim, part, place, lane, strips):
    turn = (part + 2 * DEPTH + STRIP * place) % LANES
    in_place = (lane >= STRIP * place) & (lane < STRIP * (place + 1))
    return jnp.where(in_place, pltpu.roll(rim, turn, 1), strips)


def lay_twice(source, lines, start, size, groups):
    for block in range(groups):
        value = source[block]
        for target in (block + 1, block + 1 + groups):
            lines[target, pl.ds(start, size)] = value
        if block == groups - 1:
            lines[0, pl.ds(start, size)] = value


def turn_own(groups, rows, planes):
    own = rows * planes
    zone = planes * (2 * DEPTH + 2)

    def kernel(shifts, mine, out, strips_out, lines, windows, out_sem):
        lay_twice(mine, lines, 0, own, groups)
        flat = lines.reshape((2 * groups + 1) * own, LANES)
        target = windows.reshape(groups * own, LANES)
        lane = lax.broadcasted_iota(jnp.int32, (groups, LANES), 1)
        strips = [[jnp.zeros((groups, LANES), jnp.float32) for _ in range(planes)] for _ in range(2)]
        for row in range(rows):
            wide_row = row + DEPTH
            for plane in range(planes):
                line = plane * rows + row
                window, rim, part = turned_line(flat, line, own, groups, shifts[row], lane)
                target[pl.ds(line, groups, stride=own), :] = window
                strips[wide_row % 2][plane] = placed_strip(
                    rim, part, wide_row // 2, lane, strips[wide_row % 2][plane]
                )
        for plane in range(planes):
            for parity in range(2):
                strips_out[plane * 2 + parity] = strips[parity][plane]
        leave = pltpu.make_async_copy(windows, out.at[:, pl.ds(0, own)], out_sem)
        leave.start()
        leave.wait()

    return pl.pallas_call(
        kernel,
        in_specs=[pl.BlockSpec(memory_space=pltpu.SMEM), pl.BlockSpec(memory_space=pltpu.VMEM)],
        out_shape=(
            jax.ShapeDtypeStruct((groups, own + zone, LANES), jnp.float32),
            jax.ShapeDtypeStruct((2 * planes, groups, LANES), jnp.float32),
        ),
        out_specs=(pl.BlockSpec(memory_space=pl.ANY), pl.BlockSpec(memory_space=pltpu.VMEM)),
        scratch_shapes=[
            pltpu.VMEM((2 * groups + 1, own, LANES), jnp.float32),
            pltpu.VMEM((groups, own, LANES), jnp.float32),
            pltpu.SemaphoreType.DMA,
        ],
        compiler_params=pltpu.CompilerParams(vmem_limit_bytes=24 * 1024 * 1024),
        cost_estimate=pl.CostEstimate(flops=4000000, bytes_accessed=4000000, transcendentals=0),
        name="turn_own",
    )


def turn_ghost(groups, rows, planes):
    own = rows * planes
    ghost = DEPTH * planes
    zone = 3 * ghost

    def kernel(shift_tiles, low, high, strips_in, chunk, out, lines, windows, sems):
        shift_rows = shift_tiles[...]
        amounts = [shift_rows[entry, 0] for entry in range(2 * DEPTH)]
        lay_twice(low, lines, 0, ghost, groups)
        lay_twice(high, lines, ghost, ghost, groups)
        flat = lines.reshape((2 * groups + 1) * 2 * ghost, LANES)
        target = windows.reshape(3 * groups * ghost, LANES)
        lane = lax.broadcasted_iota(jnp.int32, (groups, LANES), 1)
        strips = [
            [strips_in[plane * 2 + parity] for plane in range(planes)] for parity in range(2)
        ]

        def leave(part):
            copy = pltpu.make_async_copy(
                windows.at[part], out.at[:, pl.ds(own + part * ghost, ghost)], sems.at[part]
            )
            copy.start()
            return copy

        copies = []
        for side in range(2):
            for row in range(DEPTH):
                wide_row = row + side * (rows + DEPTH)
                for plane in range(planes):
                    line = side * ghost + plane * DEPTH + row
                    window, rim, part = turned_line(
                        flat, line, 2 * ghost, groups, amounts[side * DEPTH + row], lane
                    )
                    place = side * groups * ghost + plane * DEPTH + row
                    target[pl.ds(place, groups, stride=ghost), :] = window
                    strips[wide_row % 2][plane] = placed_strip(
                        rim, part, wide_row // 2, lane, strips[wide_row % 2][plane]
                    )
            copies.append(leave(side))
        for plane in range(planes):
            for parity in range(2):
                place = 2 * groups * ghost + plane * DEPTH + parity
                target[pl.ds(place, groups, stride=ghost), :] = strips[parity][plane]
        copies.append(leave(2))
        for copy in copies:
            copy.wait()

    return pl.pallas_call(
        kernel,
        in_specs=[pl.BlockSpec(memory_space=pltpu.VMEM)] * 4
        + [pl.BlockSpec(memory_space=pl.ANY)],
        out_shape=jax.ShapeDtypeStruct((groups, own + zone, LANES), jnp.float32),
        out_specs=pl.BlockSpec(memory_space=pl.ANY),
        input_output_aliases={4: 0},
        scratch_shapes=[
            pltpu.VMEM((2 * groups + 1, 2 * ghost, LANES), jnp.float32),
            pltpu.VMEM((3, groups, ghost, LANES), jnp.float32),
            pltpu.SemaphoreType.DMA((3,)),
        ],
        compiler_params=pltpu.CompilerParams(vmem_limit_bytes=24 * 1024 * 1024),
        name="turn_ghost",
    )


def y_up(tile):
    return pltpu.roll(tile, LANES - 1, 1)


def y_dn(tile):
    return pltpu.roll(tile, 1, 1)


def z_up(tile):
    return pltpu.roll(tile, tile.shape[0] - 1, 0)


def z_dn(tile):
    return pltpu.roll(tile, 1, 0)


def both_sides(row):
    return [y_dn(field) for field in row], [y_up(field) for field in row]


def radial_edges(prev, here, residual_prev, residual, left_prev, left):
    _, vel_x, _, vel_z, _, mag_x, mag_y, mag_z = here
    two_x = vel_x + prev[1]
    two_z = vel_z + prev[3]
    two_w = (here[2] + residual) + (prev[2] + residual_prev)
    four_x = two_x + (left[1] + left_prev[1])
    four_w = two_w + ((left[2] + left_prev[2]) + (residual + residual_prev))
    mag_x_z = z_dn(mag_x)
    emf_z = (0.125 * time_step) * (four_w * (mag_x + left[5]) - four_x * (mag_y + prev[6])) + (time_step * resist) * (
        (mag_y - prev[6]) - (mag_x - left[5])
    )
    emf_y = (0.125 * time_step) * (
        (two_x + z_dn(two_x)) * (mag_z + prev[7]) - (two_z + z_dn(two_z)) * (mag_x + mag_x_z)
    ) + (time_step * resist) * ((mag_x - mag_x_z) - (mag_z - prev[7]))
    return emf_z, emf_y


def row_step(prev, here, after, residual, ahead_prev, sides, sides_after, edges, edges_after):
    left, right = sides
    left_after, right_after = sides_after
    log_rho, vel_x, vel_y, vel_z, entropy, mag_x, mag_y, mag_z = here
    drift = vel_y + residual
    half_x = (0.5 * time_step) * vel_x
    half_w = (0.5 * time_step) * drift
    half_z = (0.5 * time_step) * vel_z

    def moved_by(index):
        center = here[index]
        fore, back = after[index], prev[index]
        behind, ahead = left[index], right[index]
        under, over = z_dn(center), z_up(center)
        d_x, d_y, d_z = fore - back, ahead - behind, over - under
        total = ((fore + back) + (behind + ahead)) + (under + over)
        result = (time_step * viscous) * total + (1.0 - 6.0 * time_step * viscous) * center
        result = result - (half_x * d_x + half_w * d_y + half_z * d_z)
        return result, d_x, d_y, d_z

    next_l, l_x, l_y, l_z = moved_by(0)
    next_vx, vx_x, _, _ = moved_by(1)
    next_vy, _, vy_y, _ = moved_by(2)
    next_vz, _, _, vz_z = moved_by(3)
    next_s, s_x, s_y, s_z = moved_by(4)

    two_bx = mag_x + after[5]
    two_by = mag_y + right[6]
    two_bz = mag_z + z_up(mag_z)
    two_bx_left = left[5] + left_after[5]
    mag_z_y = left[7]
    diff_y = after[6] - prev[6]
    diff_z = after[7] - prev[7]
    side_z = right[7] - mag_z_y
    cur_x = (side_z + z_up(side_z)) - (z_up(two_by) - z_dn(two_by))
    cur_y = (z_up(two_bx) - z_dn(two_bx)) - (diff_z + z_up(diff_z))
    cur_z = (diff_y + two_bx_left) + (
        (right_after[6] - ahead_prev) - (right[5] + right_after[5])
    )
    inverse = jnp.exp(-log_rho)
    eighth = (0.125 * time_step) * inverse
    next_l = next_l - (0.5 * time_step) * (vx_x + vy_y + vz_z)
    next_vx = (
        next_vx
        - (0.5 * time_step * sound_sq) * (l_x + s_x)
        + eighth * (cur_y * two_bz - cur_z * two_by)
        + (2.0 * time_step * rotation) * vel_y
    )
    next_vy = (
        next_vy
        - (0.5 * time_step * sound_sq) * (l_y + s_y)
        + eighth * (cur_z * two_bx - cur_x * two_bz)
        - (time_step * (2.0 - shear_rate) * rotation) * vel_x
    )
    next_vz = (
        next_vz
        - (0.5 * time_step * sound_sq) * (l_z + s_z)
        + eighth * (cur_x * two_by - cur_y * two_bx)
    )
    next_s = next_s + (0.0625 * time_step * resist) * inverse * (cur_x * cur_x + cur_y * cur_y + cur_z * cur_z)

    emf_z, emf_y = edges
    emf_z_after, emf_y_after = edges_after
    pair_w = (drift + residual) + left[2]
    pair_z = vel_z + left[3]
    mag_y_z = z_dn(mag_y)
    emf_x = (0.125 * time_step) * (
        (pair_z + z_dn(pair_z)) * (mag_y + mag_y_z) - (pair_w + z_dn(pair_w)) * (mag_z + mag_z_y)
    ) + (time_step * resist) * ((mag_z - mag_z_y) - (mag_y - mag_y_z))
    next_bx = (mag_x + emf_z) + (z_up(emf_y) - emf_y)
    next_by = (
        mag_y
        + (emf_x - z_up(emf_x))
        + (emf_z_after - emf_z)
        - (0.25 * time_step * shear_rate * rotation) * (two_bx + two_bx_left)
    )
    next_bz = (mag_z - emf_x) + (emf_y - emf_y_after)
    done = [next_l, next_vx, next_vy, next_vz, next_s, next_by]
    return done, (next_bx, emf_z, next_bz, emf_x)


DONE = (0, 1, 2, 3, 4, 6)


def last_edges(pending):
    next_bx, emf_z, next_bz, emf_x = pending
    return next_bx - y_up(emf_z), next_bz + y_up(emf_x)


def drift_tiles(drift, depth):
    wide = drift.shape[0]
    pairs = jnp.broadcast_to(drift.reshape(wide // 2, 2, 1), (wide // 2, 2, STRIP))
    strips = jnp.pad(
        jnp.swapaxes(pairs, 0, 1).reshape(2, wide // 2 * STRIP),
        ((0, 0), (0, LANES - wide // 2 * STRIP)),
    )
    strips = jnp.stack(
        [jnp.roll(strips[1], STRIP), strips[0], strips[1], jnp.roll(strips[0], -STRIP)]
    )
    tiles = jnp.concatenate([jnp.broadcast_to(drift[:, None], (wide, LANES)), strips])
    return jnp.broadcast_to(tiles[:, None], (wide + 4, depth, LANES))


def two_sections(fields, depth, rows):
    wide = rows + 2 * DEPTH
    half = depth // 2
    own = half * rows
    ghost = half * DEPTH
    chunk = own + 3 * ghost
    strip_at = wide

    def kernel(drift_rows, source, out, moved, first, whole, evolved, sems):
        flat_out = evolved.reshape(fields * depth * rows, LANES)
        lane = lax.broadcasted_iota(jnp.int32, (depth, LANES), 1)

        def widen_strips(ref):
            for field in range(fields):
                even = ref[field, strip_at + 1]
                odd = ref[field, strip_at + 2]
                ref[field, strip_at] = pltpu.roll(odd, STRIP, 1)
                ref[field, strip_at + 3] = pltpu.roll(even, LANES - STRIP, 1)

        under = lax.broadcasted_iota(jnp.int32, (depth, LANES), 0) < half

        def column(first, stride):
            return jnp.where(
                under,
                source[pl.ds(first, depth, stride=stride), :],
                source[pl.ds(first + chunk - half * stride, depth, stride=stride), :],
            )

        for field in range(fields):
            start = 2 * field * chunk
            for row in range(rows):
                moved[field, row + DEPTH] = column(start + row, rows)
            for entry in range(DEPTH):
                first_at = start + own + entry
                moved[field, entry] = column(first_at, DEPTH)
                moved[field, DEPTH + rows + entry] = column(first_at + ghost, DEPTH)
                moved[field, strip_at + 1 + entry] = column(first_at + 2 * ghost, DEPTH)
        widen_strips(moved)

        def row_of(ref, row):
            return [ref[field, row] for field in range(fields)]

        def begin(ref, row):
            prev, here = row_of(ref, row - 1), row_of(ref, row)
            sides_prev, sides = both_sides(prev), both_sides(here)
            edges = radial_edges(
                prev,
                here,
                drift_rows[row - 1],
                drift_rows[row],
                sides_prev[0],
                sides[0],
            )
            return sides_prev[1][6], sides, edges, (here[5], here[5], here[7], here[7])

        def step(ref, row, carried):
            ahead_prev, sides, edges, _ = carried
            prev, here, after = row_of(ref, row - 1), row_of(ref, row), row_of(ref, row + 1)
            drift, drift_after = drift_rows[row], drift_rows[row + 1]
            sides_after = both_sides(after)
            edges_after = radial_edges(here, after, drift, drift_after, sides[0], sides_after[0])
            done, pending = row_step(
                prev, here, after, drift_rows[row], ahead_prev, sides, sides_after, edges, edges_after
            )
            return done, (sides[1][6], sides_after, edges_after, pending)

        def settle_first(row, carried):
            first[5, row], first[7, row] = last_edges(carried[3])

        def first_row(row, carried):
            settle_first(row - 1, carried)
            done, carried = step(moved, row, carried)
            for field, value in zip(DONE, done):
                first[field, row] = value
            return carried

        carried = begin(moved, strip_at + 1)
        for row in (strip_at + 1, strip_at + 2):
            carried = first_row(row, carried)
        settle_first(strip_at + 2, carried)
        widen_strips(first)
        carried = lax.fori_loop(1, wide - 1, first_row, begin(moved, 1), unroll=wide - 2)
        settle_first(wide - 2, carried)

        def settle_second(row, carried):
            for field, value in zip((5, 7), last_edges(carried[3])):
                whole[field, row] = 0.5 * (moved[field, row] + value)

        def second_row(row, carried):
            settle_second(row - 1, carried)
            done, carried = step(first, row, carried)
            for field, value in zip(DONE, done):
                whole[field, row] = 0.5 * (moved[field, row] + value)
            return carried

        carried = begin(first, strip_at + 1)
        for row in (strip_at + 1, strip_at + 2):
            carried = second_row(row, carried)
        settle_second(strip_at + 2, carried)

        carried = begin(first, DEPTH)
        copies = []
        for block in range(rows // TILE_ROWS):
            start = DEPTH + block * TILE_ROWS
            carried = lax.fori_loop(start, start + TILE_ROWS, second_row, carried, unroll=TILE_ROWS)
            settle_second(start + TILE_ROWS - 1, carried)
            for field in range(fields):
                for row in range(start, start + TILE_ROWS):
                    turn = (LANES - 3 * DEPTH - STRIP * (row // 2)) % LANES
                    end = pltpu.roll(whole[field, strip_at + 1 + row % 2], turn, 1)
                    flat_out[pl.ds(field * depth * rows + row - DEPTH, depth, stride=rows), :] = (
                        jnp.where(
                            lane < LANES - 2 * DEPTH,
                            pltpu.roll(whole[field, row], LANES - DEPTH, 1),
                            end,
                        )
                    )
                piece = (pl.ds(field * depth, depth), pl.ds(block * TILE_ROWS, TILE_ROWS))
                copy = pltpu.make_async_copy(evolved.at[piece], out.at[piece], sems.at[block, field])
                copy.start()
                copies.append(copy)
        for copy in copies:
            copy.wait()

    return pl.pallas_call(
        kernel,
        in_specs=[pl.BlockSpec(memory_space=pltpu.VMEM), pl.BlockSpec(memory_space=pltpu.VMEM)],
        out_shape=jax.ShapeDtypeStruct((fields * depth, rows, LANES), jnp.float32),
        out_specs=pl.BlockSpec(memory_space=pl.ANY),
        scratch_shapes=[
            pltpu.VMEM((fields, wide + 4, depth, LANES), jnp.float32),
            pltpu.VMEM((fields, wide + 4, depth, LANES), jnp.float32),
            pltpu.VMEM((fields, wide + 4, depth, LANES), jnp.float32),
            pltpu.VMEM((fields * depth, rows, LANES), jnp.float32),
            pltpu.SemaphoreType.DMA((rows // TILE_ROWS, fields)),
        ],
        compiler_params=pltpu.CompilerParams(vmem_limit_bytes=24 * 1024 * 1024),
        name="two_sections",
    )


def local(state, residual, shift_rows, shear_offset):
    fields, depth, rows, cols = state.shape
    groups = lax.axis_size("gy")
    radial_count = lax.axis_size("gx")
    row_dev = lax.axis_index("gx")
    cells_y = cols * groups
    planes = fields * depth // groups
    offset = shear_offset[0]

    lines = lax.all_to_all(
        state.reshape(groups, planes, rows, cols), "gy", split_axis=0, concat_axis=0, tiled=True
    )
    low = passed_along(lines[:, :, rows - DEPTH :], "gx", 1)
    high = passed_along(lines[:, :, :DEPTH], "gx", -1)
    low_shift = passed_along(shift_rows[rows - DEPTH :], "gx", 1)
    high_shift = passed_along(shift_rows[:DEPTH], "gx", -1)
    across = jnp.ones((1, cols), jnp.int32)
    ghost_shifts = jnp.concatenate(
        [
            (low_shift - jnp.where(row_dev == 0, offset, 0))[:, None] * across,
            (high_shift + jnp.where(row_dev == radial_count - 1, offset, 0))[:, None] * across,
        ]
    )
    ghost_shifts = (ghost_shifts + DEPTH) % cells_y
    own_shifts = shift_rows + DEPTH
    chunk, strips = turn_own(groups, rows, planes)(
        own_shifts % cells_y, lines.reshape(groups, planes * rows, cols)
    )
    chunk = turn_ghost(groups, rows, planes)(
        ghost_shifts,
        low.reshape(groups, planes * DEPTH, cols),
        high.reshape(groups, planes * DEPTH, cols),
        strips,
        chunk,
    )
    wide = lax.all_to_all(chunk, "gy", split_axis=0, concat_axis=0, tiled=True)
    padded = jnp.concatenate([residual[-DEPTH:], residual, residual[:DEPTH]])
    drift = lax.dynamic_slice_in_dim(padded, row_dev * rows, rows + 2 * DEPTH)
    evolved = two_sections(fields, depth, rows)(
        drift_tiles(drift, depth), wide.reshape(-1, cols)
    )
    return evolved.reshape(state.shape)


def solution(mesh):
    return jax.shard_map(
        local,
        mesh=mesh,
        in_specs=(P(None, None, "gx", "gy"), P(), P("gx"), P()),
        out_specs=P(None, None, "gx", "gy"),
        check_vma=False,
    )
```
